32 devices in a mesh: section: 2 (over x), row: 2 (over y), col: 8 (over z, core).
Axes of the slice: x: 2, y: 2, z: 4, core: 2. Of those that a mesh axis runs over, the one named last changes fastest.
Arguments:
- images: bfloat16 [2, 2, 48, 32, 256], P('section', None, None, 'row', 'col'), may hold values from -6 to 6
- stem_first: bfloat16 [48, 256], replicated, may hold values from -0.875 to 0.875
- stem_conv: bfloat16 [3, 3, 256, 256], replicated, may hold values from -0.125 to 0.125
- patch_weight: bfloat16 [4096, 1024], P('col'), may hold values from -0.09375 to 0.09375
- position: bfloat16 [64, 8, 1024], P('col', 'row'), may hold values from -6 to 6
- gain_attn: float32 [1024], replicated, may hold values from 0.1 to 1.9
- w_qkv: bfloat16 [3, 1024, 1024], P(None, None, 'col'), may hold values from -0.5 to 0.5
- w_out: bfloat16 [1024, 1024], P('col'), may hold values from -0.1875 to 0.1875
- gain_mlp: float32 [1024], replicated, may hold values from 0.1 to 1.9
- w_up: bfloat16 [1024, 4096], P(None, 'col'), may hold values from -0.1875 to 0.1875
- w_down: bfloat16 [4096, 1024], P('col'), may hold values from -0.09375 to 0.09375
Outputs:
- encoded: bfloat16 [2, 2, 64, 8, 1024], P('section', 'row', 'col')
The draws below stay inside these ranges and needn't reach their ends.
All inputs are finite; a program needn't handle non-finite values.
Results may differ from the reference program's by a relative error of at most 0.024.
The reference program's roundings to bfloat16 on the way count: a program that leaves them out, or rounds other values in their place, can miss the bound.
Values may be sent and summed in bfloat16 or wider, within the bound.
A program may use at most 64 MiB of HBM per device.

```python
import jax
import jax.numpy as jnp
from jax import lax

D = 1024
HEADS = 16
HD = 64
FF = 4096
C = 256
TCOLS = 64
PF = 4096
TROWS = 8
IMGS = 2
MB = 2
N_COL = 8


def block_levels(own_key, shape, split, low, top_value):
    gain, own = 1.0, jax.random.fold_in(own_key, 6)
    for dim, blocks in split:
        heights = jnp.exp(jax.random.uniform(jax.random.fold_in(own, dim), (blocks,), jnp.float32, low / len(split), top_value / len(split)))
        gain = gain * jnp.repeat(heights, shape[dim] // blocks).reshape([-1 if axis == dim else 1 for axis in range(len(shape))])
    return gain


def noise(key, extent, deviation, bound, cuts=(), dtype=jnp.bfloat16):
    array = jax.random.normal(key, extent, jnp.float32) * deviation
    if len(cuts) > 0:
        array = block_levels(key, extent, cuts, -0.22, 0.18) * array
    return jnp.clip(array, min=-bound, max=bound).astype(dtype)


def setup_inputs(seed: int = 0) -> dict:
    splits = jax.random.split(jax.random.key(seed), 12)
    return {
        "images": noise(splits[0], (MB, IMGS, 48, 4 * TROWS, 4 * TCOLS), 1.0, 6.0, ((0, 2), (3, 2), (4, 8))),
        "stem_first": noise(splits[1], (48, C), 48 ** -0.5, 0.875),
        "stem_conv": noise(splits[2], (3, 3, C, C), (9 * C) ** -0.5, 0.125),
        "patch_weight": noise(splits[3], (PF, D), PF ** -0.5, 0.09375, ((0, 8),)),
        "position": noise(splits[4], (TCOLS, TROWS, D), 1.0, 6.0, ((0, 8), (1, 2))),
        "gain_attn": jnp.clip(1.0 + 0.18 * jax.random.normal(splits[5], (D,), jnp.float32), 0.1, 1.9),
        "w_qkv": noise(splits[6], (3, D, HEADS * HD), (D // 8) ** -0.5, 0.5, ((2, 8),)),
        "w_out": noise(splits[7], (HEADS * HD, D), (HEADS * HD) ** -0.5, 0.1875, ((0, 8),)),
        "gain_mlp": jnp.clip(1.0 + 0.18 * jax.random.normal(splits[8], (D,), jnp.float32), 0.1, 1.9),
        "w_up": noise(splits[9], (D, FF), D ** -0.5, 0.1875, ((1, 8),)),
        "w_down": noise(splits[10], (FF, D), FF ** -0.5, 0.09375, ((0, 8),)),
    }


def layer_norm(vectors, gain_vec):
    row_mean = lax.optimization_barrier(jnp.mean(vectors, axis=-1, keepdims=True))
    center = vectors - row_mean
    spread = lax.optimization_barrier(jnp.mean(center * center, axis=-1, keepdims=True))
    return center * lax.rsqrt(spread + 1e-06) * gain_vec.astype(jnp.float32)

def stem_image(pixels, stem_first, stem_conv):
    first_map = jnp.einsum('khw,kc->hwc', pixels.astype(jnp.float32), stem_first.astype(jnp.float32))
    stem_maps = jnp.maximum(first_map, 0.0).astype(jnp.bfloat16)
    padded = jnp.pad(stem_maps, ((1, 1), (1, 1), (0, 0)))
    height = stem_maps.shape[0]
    tile_width = stem_maps.shape[1]
    summed = stem_maps.astype(jnp.float32)
    for offset_a in range(3):
        for offset_b in range(3):
            window = padded[offset_a:offset_a + height, offset_b:offset_b + tile_width, :].astype(jnp.float32)
            summed = summed + jnp.einsum('hwc,cd->hwd', window, stem_conv[offset_a, offset_b].astype(jnp.float32))
    deep_maps = jnp.maximum(summed, 0.0).astype(jnp.bfloat16)
    blocks = deep_maps.reshape(height // 4, 4, tile_width // 4, 4, C).transpose(2, 0, 1, 3, 4)
    return blocks.reshape(height // 4 * (tile_width // 4), 16 * C)

def group_sum(left, right_side):
    group_width = left.shape[1] // N_COL
    left_groups = left.reshape(left.shape[0], N_COL, group_width).astype(jnp.float32)
    right_groups = right_side.reshape(N_COL, group_width, right_side.shape[1]).astype(jnp.float32)
    terms = jnp.einsum('tgh,ghd->gtd', left_groups, right_groups).astype(jnp.bfloat16)
    terms = lax.optimization_barrier(terms)
    return lax.optimization_barrier(jnp.sum(terms.astype(jnp.float32), axis=0))

def encoder_layer(embedded, gain_attn, w_qkv, w_out, gain_mlp, w_up, w_down):
    residual = embedded.astype(jnp.float32)
    normed = layer_norm(residual, gain_attn).astype(jnp.bfloat16)
    projected = jnp.einsum('td,kdh->kth', normed.astype(jnp.float32), w_qkv.astype(jnp.float32)).astype(jnp.bfloat16)
    token_count = embedded.shape[0]
    split_heads = projected.reshape(3, token_count, HEADS, HD).transpose(0, 2, 1, 3)

    def one_head(triple):
        queries, key_rows, value_rows = triple
        scores = jnp.einsum('qd,kd->qk', queries.astype(jnp.float32), key_rows.astype(jnp.float32)) * HD ** (-0.5)
        row_peak = lax.optimization_barrier(jnp.max(scores, axis=-1, keepdims=True))
        expo = jnp.exp(scores - row_peak)
        prob_rows = (expo / lax.optimization_barrier(jnp.sum(expo, axis=-1, keepdims=True))).astype(jnp.bfloat16)
        return jnp.einsum('qk,kd->qd', prob_rows.astype(jnp.float32), value_rows.astype(jnp.float32)).astype(jnp.bfloat16)
    attended = lax.map(one_head, (split_heads[0], split_heads[1], split_heads[2]))
    mixed_heads = attended.transpose(1, 0, 2).reshape(token_count, HEADS * HD)
    after = residual + group_sum(mixed_heads, w_out)
    normed_mlp = layer_norm(after, gain_mlp).astype(jnp.bfloat16)
    hidden = jax.nn.gelu(jnp.dot(normed_mlp, w_up, preferred_element_type=jnp.float32), approximate=True).astype(jnp.bfloat16)
    return (after + group_sum(hidden, w_down)).astype(jnp.bfloat16)

def reference(images, stem_first, stem_conv, patch_weight, position, gain_attn, w_qkv, w_out, gain_mlp, w_up, w_down):
    flat_images = images.reshape(MB * IMGS, 48, 4 * TROWS, 4 * TCOLS)
    position_rows = position.reshape(TCOLS * TROWS, D).astype(jnp.float32)

    def one_image(pixels):
        features = stem_image(pixels, stem_first, stem_conv)
        embedded = (jnp.dot(features, patch_weight, preferred_element_type=jnp.float32) + position_rows).astype(jnp.bfloat16)
        return encoder_layer(embedded, gain_attn, w_qkv, w_out, gain_mlp, w_up, w_down)
    results = lax.map(one_image, flat_images)
    results = results.reshape(MB, IMGS, TCOLS, TROWS, D)
    return jnp.roll(results, 1, axis=0)
```

```python
import functools
import math

import jax
import jax.numpy as jnp
from jax import lax
from jax.experimental import pallas as pl
from jax.experimental.pallas import tpu as pltpu
from jax.sharding import PartitionSpec as P

HD = 64
V = pltpu.VMEM


def call(body, out, ins, scratch, cid, name, **kw):
    return pl.pallas_call(body, out_shape=out,
        in_specs=[pl.BlockSpec(memory_space=pltpu.VMEM)]*len(ins),
        out_specs=jax.tree.map(lambda _: pl.BlockSpec(memory_space=pltpu.VMEM), out),
        scratch_shapes=scratch, name=name,
        compiler_params=pltpu.CompilerParams(collective_id=cid, has_side_effects=True, vmem_limit_bytes=48<<20))(*ins)


def rc(src, dst, ss, rs, **dev):
    return pltpu.make_async_remote_copy(src_ref=src, dst_ref=dst, send_sem=ss, recv_sem=rs, device_id=dev, device_id_type=pl.DeviceIdType.MESH)


def greet(devs):
    b = pltpu.get_barrier_semaphore()
    for d in devs:
        pl.semaphore_signal(b, inc=1, device_id=d, device_id_type=pl.DeviceIdType.MESH)
    pl.semaphore_wait(b, len(devs))


def ag_hier(x, cid):
    n = lax.axis_size("col"); zs = n//2
    def body(x_ref, o_ref, s1, s2, r1, r2, sp, rp, ls):
        me = lax.axis_index("col"); z = me//2; p = lax.rem(me,2); mate = me+1-2*p
        far = [lax.rem(me+2*k, n) for k in range(1, zs)]
        greet([{"col": mate}]+[{"col": d} for d in far])
        cs=[]
        for k in range(1,zs):
            c = rc(x_ref, o_ref.at[me], s1.at[k], r1.at[zs-k], col=far[k-1]); c.start(); cs.append(c)
        c = rc(x_ref, o_ref.at[me], sp, rp, col=mate); c.start(); cs.append(c)
        l = pltpu.make_async_copy(x_ref, o_ref.at[me], ls); l.start()
        order = sorted(range(1,zs), key=lambda k: min(k, zs-k))
        for k in order:
            src = far[k-1]
            rc(x_ref, o_ref.at[src], s1.at[k], r1.at[k], col=mate).wait_recv()
            c = rc(o_ref.at[src], o_ref.at[src], s2.at[k], r2.at[k], col=mate); c.start(); cs.append(c)
        l.wait()
        rc(x_ref, o_ref.at[mate], sp, rp, col=mate).wait_recv()
        for k in order:
            src = lax.rem(mate+2*k, n)
            rc(x_ref, o_ref.at[src], s2.at[k], r2.at[k], col=mate).wait_recv()
        for c in cs: c.wait_send()
    D=pltpu.SemaphoreType.DMA
    return call(body, jax.ShapeDtypeStruct((n,)+x.shape, x.dtype), [x], [D((zs,)),D((zs,)),D((zs,)),D((zs,)),D,D,D], cid, "aghier%d"%cid)


def rs_hier(parts, cid):
    n = lax.axis_size("col"); zs = n//2
    blk = parts.shape[1:]
    def body(x_ref, o_ref, buf1, stage, buf2, s1, r1, s2, r2):
        me = lax.axis_index("col"); z = me//2; p = lax.rem(me,2); mate = me+1-2*p
        far = [lax.rem(me+2*k, n) for k in range(zs)]
        matefar = [lax.rem(mate+2*k, n) for k in range(zs)]
        greet([{"col": mate}]+[{"col": d} for d in far[1:]])
        order = sorted(range(1,zs), key=lambda k: -min(k, zs-k)) + [0]
        cs=[]
        for k in order:
            c = rc(x_ref.at[matefar[k]], buf1.at[k], s1.at[k], r1.at[k], col=mate); c.start(); cs.append(c)
        for k in order:
            rc(x_ref.at[0], buf1.at[k], s1.at[k], r1.at[k], col=mate).wait_recv()
            tot = x_ref[far[k]].astype(jnp.float32) + buf1[k].astype(jnp.float32)
            if k:
                stage[k] = tot.astype(stage.dtype)
                c = rc(stage.at[k], buf2.at[zs-k], s2.at[k], r2.at[zs-k], col=far[k]); c.start(); cs.append(c)
        for k in order[::-1][1:]:
            rc(stage.at[0], buf2.at[k], s2.at[k], r2.at[k], col=mate).wait_recv()
            tot = tot + buf2[k].astype(jnp.float32)
        o_ref[...] = tot
        for c in cs: c.wait_send()
    D=pltpu.SemaphoreType.DMA
    return call(body, jax.ShapeDtypeStruct(blk, jnp.float32), [parts], [V((zs,)+blk, parts.dtype)]*3+[D((zs,)),D((zs,)),D((zs,)),D((zs,))], cid, "rshier%d"%cid)


def a2a_col(x, cid):
    n = lax.axis_size("col")

    def body(x_ref, o_ref, ss, rs, ls):
        me = lax.axis_index("col")
        greet([{"col": lax.rem(me + k, n)} for k in range(1, n)])
        cs = []
        for k in range(1, n):
            d = lax.rem(me + k, n)
            c = rc(x_ref.at[d], o_ref.at[me], ss.at[k], rs.at[n - k], col=d)
            c.start()
            cs.append(c)
        own = pltpu.make_async_copy(x_ref.at[me], o_ref.at[me], ls)
        own.start()
        own.wait()
        for k in range(1, n):
            d = lax.rem(me + k, n)
            rc(x_ref.at[d], o_ref.at[d], ss.at[k], rs.at[k], col=d).wait_recv()
        for c in cs:
            c.wait_send()

    D = pltpu.SemaphoreType.DMA
    return call(
        body, jax.ShapeDtypeStruct(x.shape, x.dtype), [x], [D((n,)), D((n,)), D], cid, "spread"
    )


def swap_groups(x, cid):
    count = lax.axis_size("row")
    secs = lax.axis_size("section")

    def body(x_ref, o_ref, ss, rs):
        s, r = lax.axis_index("section"), lax.axis_index("row")
        to = lax.rem(s + 1, secs)
        back = lax.rem(s + secs - 1, secs)
        b = pltpu.get_barrier_semaphore()
        for k in range(count):
            pl.semaphore_signal(
                b,
                inc=1,
                device_id={"section": back, "row": lax.rem(r + k, count)},
                device_id_type=pl.DeviceIdType.MESH,
            )
        pl.semaphore_wait(b, count)
        cs = []
        for k in range(count):
            d = lax.rem(r + k, count)
            c = rc(x_ref.at[d], o_ref.at[r], ss.at[k], rs.at[(count - k) % count], section=to, row=d)
            c.start()
            cs.append(c)
        for k in range(count):
            d = lax.rem(r + k, count)
            rc(x_ref.at[d], o_ref.at[d], ss.at[k], rs.at[k], section=to, row=d).wait_recv()
        for c in cs:
            c.wait_send()

    D = pltpu.SemaphoreType.DMA
    return call(
        body, jax.ShapeDtypeStruct(x.shape, x.dtype), [x], [D((count,)), D((count,))], cid, "swap"
    )


def halo(first, cid):
    imgs, height, width, ch = first.shape
    rows_n, cols_n = lax.axis_size("row"), lax.axis_size("col")
    steps = [(a, b) for a in (-1, 0, 1) for b in (-1, 0, 1) if (a, b) != (0, 0)]
    edge = {-1: slice(0, 1), 0: slice(None), 1: slice(-1, None)}
    ins = [first[:, edge[a], edge[b], :].reshape(-1, ch) for a, b in steps]

    def body(*refs):
        src, dst = refs[:8], refs[8:16]
        ss, rs = refs[16:]
        r, c = lax.axis_index("row"), lax.axis_index("col")
        bar = pltpu.get_barrier_semaphore()

        def there(a, b):
            ok = jnp.int32(1)
            if a == -1:
                ok = ok * (r > 0).astype(jnp.int32)
            if a == 1:
                ok = ok * (r < rows_n - 1).astype(jnp.int32)
            if b == -1:
                ok = ok * (c > 0).astype(jnp.int32)
            if b == 1:
                ok = ok * (c < cols_n - 1).astype(jnp.int32)
            return ok

        have = [there(a, b) for a, b in steps]
        total = functools.reduce(lambda p, q: p + q, have)
        for (a, b), ok in zip(steps, have):

            @pl.when(ok == 1)
            def _():
                pl.semaphore_signal(
                    bar,
                    inc=1,
                    device_id={"row": r + a, "col": c + b},
                    device_id_type=pl.DeviceIdType.MESH,
                )

        pl.semaphore_wait(bar, total)
        for i, ((a, b), ok) in enumerate(zip(steps, have)):

            @pl.when(ok == 1)
            def _():
                rc(src[i], dst[7 - i], ss.at[i], rs.at[7 - i], row=r + a, col=c + b).start()

            @pl.when(ok == 0)
            def _():
                dst[i][...] = jnp.zeros_like(dst[i])

        for i, ((a, b), ok) in enumerate(zip(steps, have)):

            @pl.when(ok == 1)
            def _():
                desc = rc(src[i], dst[i], ss.at[i], rs.at[i], row=r + a, col=c + b)
                desc.wait_recv()
                desc.wait_send()

    D = pltpu.SemaphoreType.DMA
    outs = call(
        body,
        tuple(jax.ShapeDtypeStruct(v.shape, v.dtype) for v in ins),
        ins,
        [D((8,)), D((8,))],
        cid,
        "halo",
    )
    got = {}
    for (a, b), v in zip(steps, outs):
        got[a, b] = v.reshape(imgs, height if a == 0 else 1, width if b == 0 else 1, ch)
    got[0, 0] = first
    return jnp.concatenate(
        [jnp.concatenate([got[a, b] for b in (-1, 0, 1)], axis=2) for a in (-1, 0, 1)], axis=1
    )


def layer_norm(vectors, gain_vec):
    row_mean = jnp.mean(vectors, axis=-1, keepdims=True)
    center = vectors - row_mean
    spread = jnp.mean(center * center, axis=-1, keepdims=True)
    return center * lax.rsqrt(spread + 1e-06) * gain_vec


def stem_features(images, stem_first, stem_conv):
    pixels = images[0]
    first_map = jnp.einsum("ikhw,kc->ihwc", pixels, stem_first, preferred_element_type=jnp.float32)
    stem_maps = jnp.maximum(first_map, 0.0).astype(jnp.bfloat16)
    padded = halo(stem_maps, 0)
    img_count, height, tile_width, channels = stem_maps.shape
    summed = stem_maps.astype(jnp.float32)
    for offset_a in range(3):
        for offset_b in range(3):
            window = padded[:, offset_a : offset_a + height, offset_b : offset_b + tile_width, :]
            summed = summed + jnp.einsum(
                "ihwc,cd->ihwd",
                window,
                stem_conv[offset_a, offset_b],
                preferred_element_type=jnp.float32,
            )
    deep_maps = jnp.maximum(summed, 0.0).astype(jnp.bfloat16)
    blocks = deep_maps.reshape(img_count, height // 4, 4, tile_width // 4, 4, channels).transpose(
        0, 3, 1, 2, 4, 5
    )
    return blocks.reshape(img_count, tile_width // 4, height // 4, 16 * channels)


def on_device(
    images,
    stem_first,
    stem_conv,
    patch_weight,
    position,
    gain_attn,
    w_qkv,
    w_out,
    gain_mlp,
    w_up,
    w_down,
):
    features = stem_features(images, stem_first, stem_conv)
    img_count, cols_here, rows_here, feat_width = features.shape
    model_width = patch_weight.shape[1]
    flat_local = features.reshape(-1, feat_width)
    n = lax.axis_size("col")
    rows_n = lax.axis_size("row")
    here = flat_local.shape[0]
    pieces = a2a_col(flat_local.reshape(here, n, -1).transpose(1, 0, 2), 1)
    terms = jnp.dot(
        pieces.reshape(n * here, -1), patch_weight, preferred_element_type=jnp.float32
    ).astype(jnp.bfloat16)
    embedded = rs_hier(terms.reshape(n, here, model_width), 2)
    local_tokens = (
        embedded.reshape(img_count, cols_here, rows_here, model_width)
        + position.astype(jnp.float32)[None]
    ).astype(jnp.bfloat16)
    arrived = swap_groups(local_tokens.reshape(rows_n, -1, model_width), 3)
    tokens_in = (
        arrived.reshape(rows_n, img_count // rows_n, cols_here, rows_here, model_width)
        .transpose(1, 2, 0, 3, 4)
        .reshape(-1, model_width)
    )
    residual = tokens_in.astype(jnp.float32)
    normed = layer_norm(residual, gain_attn).astype(jnp.bfloat16)
    projected = jnp.einsum(
        "td,kdh->kth",
        ag_hier(normed, 4).reshape(-1, model_width),
        w_qkv,
        preferred_element_type=jnp.float32,
    ).astype(jnp.bfloat16)
    token_count = projected.shape[1]
    local_heads = w_out.shape[0] // HD
    split_heads = projected.reshape(3, token_count, local_heads, HD).transpose(0, 2, 1, 3)
    key_heads = split_heads[1]
    value_heads = split_heads[2]
    block_rows = math.gcd(token_count, 512)
    query_blocks = (
        split_heads[0]
        .reshape(local_heads, token_count // block_rows, block_rows, HD)
        .transpose(1, 0, 2, 3)
    )

    def attend(query_block):
        scores = jnp.einsum(
            "hqd,hkd->hqk", query_block, key_heads, preferred_element_type=jnp.float32
        ) * HD ** (-0.5)
        row_peak = jnp.max(scores, axis=-1, keepdims=True)
        expo = jnp.exp(scores - row_peak)
        prob_rows = (expo / jnp.sum(expo, axis=-1, keepdims=True)).astype(jnp.bfloat16)
        return jnp.einsum(
            "hqk,hkd->hqd", prob_rows, value_heads, preferred_element_type=jnp.float32
        ).astype(jnp.bfloat16)

    attended = lax.map(attend, query_blocks)
    mixed_heads = attended.transpose(0, 2, 1, 3).reshape(token_count, local_heads * HD)
    row_slice = mixed_heads
    after = residual + rs_hier(
        jnp.dot(row_slice, w_out, preferred_element_type=jnp.float32)
        .astype(jnp.bfloat16)
        .reshape(n, -1, model_width),
        5,
    )
    normed_mlp = layer_norm(after, gain_mlp).astype(jnp.bfloat16)
    hidden = jax.nn.gelu(
        jnp.dot(
            ag_hier(normed_mlp, 6).reshape(-1, model_width),
            w_up,
            preferred_element_type=jnp.float32,
        ),
        approximate=True,
    ).astype(jnp.bfloat16)
    row_slice = hidden
    encoded = (
        after
        + rs_hier(
        jnp.dot(row_slice, w_down, preferred_element_type=jnp.float32)
        .astype(jnp.bfloat16)
        .reshape(n, -1, model_width),
        7,
    )
    ).astype(jnp.bfloat16)
    return encoded.reshape(1, 1, cols_here, -1, model_width)


def solution(mesh):
    placed = (
        P("section", None, None, "row", "col"),
        P(),
        P(),
        P("col", None),
        P("col", "row", None),
        P(),
        P(None, None, "col"),
        P("col", None),
        P(),
        P(None, "col"),
        P("col", None),
    )
    return jax.shard_map(
        on_device,
        mesh=mesh,
        in_specs=placed,
        out_specs=P("section", "row", "col", None, None),
        check_vma=False,
    )
```

```python
import functools
import math

import jax
import jax.numpy as jnp
from jax import lax
from jax.experimental import pallas as pl
from jax.experimental.pallas import tpu as pltpu
from jax.sharding import PartitionSpec as P

HD = 64
V = pltpu.VMEM


def call(body, out, ins, scratch, cid, name, **kw):
    return pl.pallas_call(body, out_shape=out,
        in_specs=[pl.BlockSpec(memory_space=pltpu.VMEM)]*len(ins),
        out_specs=jax.tree.map(lambda _: pl.BlockSpec(memory_space=pltpu.VMEM), out),
        scratch_shapes=scratch, name=name,
        compiler_params=pltpu.CompilerParams(collective_id=cid, has_side_effects=True, vmem_limit_bytes=48<<20))(*ins)


def rc(src, dst, ss, rs, **dev):
    return pltpu.make_async_remote_copy(src_ref=src, dst_ref=dst, send_sem=ss, recv_sem=rs, device_id=dev, device_id_type=pl.DeviceIdType.MESH)


def greet(devs):
    b = pltpu.get_barrier_semaphore()
    for d in devs:
        pl.semaphore_signal(b, inc=1, device_id=d, device_id_type=pl.DeviceIdType.MESH)
    pl.semaphore_wait(b, len(devs))


def ag_line(x, cid, chunks=1):
    n = lax.axis_size("col"); zs = n//2
    T = x.shape[0]//chunks
    def body(x_ref, o_ref, su, sd, sm, ru, rd, rm, ls):
        me = lax.axis_index("col"); z = me//2; p = lax.rem(me,2); mate = me+1-2*p
        bar = pltpu.get_barrier_semaphore()
        def sig(d): pl.semaphore_signal(bar, inc=1, device_id={"col": d}, device_id_type=pl.DeviceIdType.MESH)
        lo = z > 0; hi = z < zs-1
        sig(mate)
        pl.when(lo)(lambda: sig(me-2)); pl.when(hi)(lambda: sig(me+2))
        pl.semaphore_wait(bar, 1 + lo.astype(jnp.int32) + hi.astype(jnp.int32))
        def part(ref, c): return ref.at[pl.ds(c*T, T)]
        def up(src, blk, c): return rc(part(src,c), part(o_ref.at[blk],c), su.at[blk//2,c], ru.at[blk//2,c], col=me+2)
        def dn(src, blk, c): return rc(part(src,c), part(o_ref.at[blk],c), sd.at[blk//2,c], rd.at[blk//2,c], col=me-2)
        def mt(src, blk, c): return rc(part(src,c), part(o_ref.at[blk],c), sm.at[blk//2,c], rm.at[blk//2,c], col=mate)
        for c in range(chunks):
            pl.when(hi)(lambda: up(x_ref, me, c).start())
            pl.when(lo)(lambda: dn(x_ref, me, c).start())
        for c in range(chunks):
            mt(x_ref, me, c).start()
        l = pltpu.make_async_copy(x_ref, o_ref.at[me], ls); l.start()
        for k in range(1, zs):
            for c in range(chunks):
                @pl.when(z-k >= 0)
                def _():
                    b = me-2*k
                    up(o_ref.at[b], b, c).wait_recv()
                    pl.when(hi)(lambda: up(o_ref.at[b], b, c).start())
                    mt(o_ref.at[b], b, c).start()
                @pl.when(z+k < zs)
                def _():
                    b = me+2*k
                    dn(o_ref.at[b], b, c).wait_recv()
                    pl.when(lo)(lambda: dn(o_ref.at[b], b, c).start())
                    mt(o_ref.at[b], b, c).start()
        l.wait()
        for j in range(zs):
            for c in range(chunks):
                b = 2*j+p
                mt(o_ref.at[b], b, c).wait_send()
                mt(o_ref.at[2*j+1-p], 2*j+1-p, c).wait_recv()
                @pl.when(hi & (j <= z))
                def _(): up(o_ref.at[b], b, c).wait_send()
                @pl.when(lo & (j >= z))
                def _(): dn(o_ref.at[b], b, c).wait_send()
    D=pltpu.SemaphoreType.DMA((zs,chunks))
    return call(body, jax.ShapeDtypeStruct((n,)+x.shape, x.dtype), [x], [D,D,D,D,D,D,pltpu.SemaphoreType.DMA], cid, "agline%d_%d"%(chunks,cid))


def rs_hier(parts, cid):
    n = lax.axis_size("col"); zs = n//2
    blk = parts.shape[1:]
    def body(x_ref, o_ref, buf1, stage, buf2, s1, r1, s2, r2):
        me = lax.axis_index("col"); z = me//2; p = lax.rem(me,2); mate = me+1-2*p
        far = [lax.rem(me+2*k, n) for k in range(zs)]
        matefar = [lax.rem(mate+2*k, n) for k in range(zs)]
        greet([{"col": mate}]+[{"col": d} for d in far[1:]])
        order = sorted(range(1,zs), key=lambda k: -min(k, zs-k)) + [0]
        cs=[]
        for k in order:
            c = rc(x_ref.at[matefar[k]], buf1.at[k], s1.at[k], r1.at[k], col=mate); c.start(); cs.append(c)
        for k in order:
            rc(x_ref.at[0], buf1.at[k], s1.at[k], r1.at[k], col=mate).wait_recv()
            tot = x_ref[far[k]].astype(jnp.float32) + buf1[k].astype(jnp.float32)
            if k:
                stage[k] = tot.astype(stage.dtype)
                c = rc(stage.at[k], buf2.at[zs-k], s2.at[k], r2.at[zs-k], col=far[k]); c.start(); cs.append(c)
        for k in order[::-1][1:]:
            rc(stage.at[0], buf2.at[k], s2.at[k], r2.at[k], col=mate).wait_recv()
            tot = tot + buf2[k].astype(jnp.float32)
        o_ref[...] = tot
        for c in cs: c.wait_send()
    D=pltpu.SemaphoreType.DMA
    return call(body, jax.ShapeDtypeStruct(blk, jnp.float32), [parts], [V((zs,)+blk, parts.dtype)]*3+[D((zs,)),D((zs,)),D((zs,)),D((zs,))], cid, "rshier%d"%cid)


def swap_groups(x, cid):
    count = lax.axis_size("row")
    secs = lax.axis_size("section")

    def body(x_ref, o_ref, ss, rs):
        s, r = lax.axis_index("section"), lax.axis_index("row")
        to = lax.rem(s + 1, secs)
        back = lax.rem(s + secs - 1, secs)
        b = pltpu.get_barrier_semaphore()
        for k in range(count):
            pl.semaphore_signal(
                b,
                inc=1,
                device_id={"section": back, "row": lax.rem(r + k, count)},
                device_id_type=pl.DeviceIdType.MESH,
            )
        pl.semaphore_wait(b, count)
        cs = []
        for k in range(count):
            d = lax.rem(r + k, count)
            c = rc(x_ref.at[d], o_ref.at[r], ss.at[k], rs.at[(count - k) % count], section=to, row=d)
            c.start()
            cs.append(c)
        for k in range(count):
            d = lax.rem(r + k, count)
            rc(x_ref.at[d], o_ref.at[d], ss.at[k], rs.at[k], section=to, row=d).wait_recv()
        for c in cs:
            c.wait_send()

    D = pltpu.SemaphoreType.DMA
    return call(
        body, jax.ShapeDtypeStruct(x.shape, x.dtype), [x], [D((count,)), D((count,))], cid, "swap"
    )


def stem_embed(first, conv, patch_weight, cid):
    imgs, height, width, ch = first.shape
    rows_n, cols_n = lax.axis_size("row"), lax.axis_size("col")
    n, zs = cols_n, cols_n // 2
    tall, deep_k = height + 2, patch_weight.shape[0]
    model = patch_weight.shape[1]
    group = width // 4
    tokens = imgs * (height // 4) * group
    f32, bf16 = jnp.float32, jnp.bfloat16
    steps = [(a, b) for a in (-1, 0, 1) for b in (-1, 0, 1) if (a, b) != (0, 0)]

    def body(
        x_ref, w_ref, p_ref, o_ref,
        row_in, col_f, col_out, col_in, cor_out, cor_in, side, shifted, deep, feat_f, feat, pieces,
        terms, near, stage, far_in,
        hs, hr, as_, ar, s1, r1, s2, r2,
    ):
        r, me = lax.axis_index("row"), lax.axis_index("col")
        z, par = me // 2, lax.rem(me, 2)
        mate = me + 1 - 2 * par
        bar = pltpu.get_barrier_semaphore()

        def there(a, b):
            ok = jnp.int32(1)
            if a == -1:
                ok = ok * (r > 0).astype(jnp.int32)
            if a == 1:
                ok = ok * (r < rows_n - 1).astype(jnp.int32)
            if b == -1:
                ok = ok * (me > 0).astype(jnp.int32)
            if b == 1:
                ok = ok * (me < cols_n - 1).astype(jnp.int32)
            return ok

        def signal(dev):
            pl.semaphore_signal(bar, inc=1, device_id=dev, device_id_type=pl.DeviceIdType.MESH)

        have = [there(a, b) for a, b in steps]
        total = jnp.int32(n - 1)
        for k in range(1, n):
            signal({"col": lax.rem(me + k, n)})
        for (a, b), ok in zip(steps, have):
            if a != 0:
                total = total + ok
                pl.when(ok == 1)(lambda: signal({"row": r + a, "col": me + b}))

        def edges(i, carry):
            v = x_ref[i].astype(f32)
            col_f[0, pl.ds(i, 1), :] = v[:1]
            col_f[1, pl.ds(i, 1), :] = v[width - 1 :]
            return carry

        lax.fori_loop(0, imgs * height, edges, 0, unroll=4)
        col_out[...] = col_f[...].astype(bf16)
        for e in range(2):
            for f in range(2):
                for i in range(imgs):
                    at = i * height + (height - 1) * e
                    side[0, i : i + 1, :] = col_f[f, at : at + 1, :]
                cor_out[2 * e + f] = side[0, :imgs, :].astype(bf16)

        def route(a, b):
            if b == 0:
                e = (a + 1) // 2
                img = x_ref.reshape(imgs, height, width, ch)
                return img.at[:, (height - 1) * e], row_in.at[1 - e], row_in.at[e]
            if a == 0:
                f = (b + 1) // 2
                return col_out.at[f], col_in.at[1 - f], col_in.at[f]
            e, f = (a + 1) // 2, (b + 1) // 2
            return cor_out.at[2 * e + f], cor_in.at[3 - 2 * e - f], cor_in.at[2 * e + f]

        pl.semaphore_wait(bar, total)
        for j, ((a, b), ok) in enumerate(zip(steps, have)):
            src, there_ref, here_ref = route(a, b)

            @pl.when(ok == 1)
            def _():
                rc(src, there_ref, hs.at[j], hr.at[7 - j], row=r + a, col=me + b).start()

            @pl.when(ok == 0)
            def _():
                here_ref[...] = jnp.zeros_like(here_ref)

        for j, ((a, b), ok) in enumerate(zip(steps, have)):
            src, there_ref, here_ref = route(a, b)

            @pl.when(ok == 1)
            def _():
                c = rc(src, here_ref, hs.at[j], hr.at[j], row=r + a, col=me + b)
                c.wait_recv()
                c.wait_send()

        for f in range(2):
            for i in range(imgs):
                base = i * tall
                side[f, base + 1 : base + 1 + height, :] = col_in[
                    f, i * height : (i + 1) * height, :
                ].astype(f32)
            for e in range(2):
                got = cor_in[2 * e + f].astype(f32)
                for i in range(imgs):
                    at = i * tall + (tall - 1) * e
                    side[f, at : at + 1, :] = got[i : i + 1]
        place = lax.broadcasted_iota(jnp.int32, (width, ch), 0)

        def put(at, v):
            v = v.astype(f32)
            left = jnp.broadcast_to(side[0, pl.ds(at, 1), :], (width, ch))
            right = jnp.broadcast_to(side[1, pl.ds(at, 1), :], (width, ch))
            shifted[0, at] = jnp.where(place == 0, left, pltpu.roll(v, 1, 0)).astype(bf16)
            shifted[1, at] = v.astype(bf16)
            shifted[2, at] = jnp.where(
                place == width - 1, right, pltpu.roll(v, width - 1, 0)
            ).astype(bf16)

        for i in range(imgs):
            put(i * tall, row_in[0, i])
            put(i * tall + tall - 1, row_in[1, i])

        for i in range(imgs):

            def fill(h, carry):
                put(i * tall + 1 + h, x_ref[i * height + h])
                return carry

            lax.fori_loop(0, height, fill, 0, unroll=4)

        part_k = deep_k // ch

        def image(i, carry):
            acc = x_ref[pl.ds(i * height, height)].reshape(height * width, ch).astype(f32)
            for a in range(3):
                for b in range(3):
                    win = shifted[b, pl.ds(i * tall + a, height)].reshape(height * width, ch)
                    acc = acc + jnp.dot(win, w_ref[a, b], preferred_element_type=f32)
            acc = jnp.maximum(acc, 0.0).astype(bf16).astype(f32)
            pixels = pl.multiple_of(i * height * width, height * width)
            for l in range(ch // 128):
                deep[l, pl.ds(pixels, height * width), :] = acc[:, 128 * l : 128 * (l + 1)]
            return carry

        lax.fori_loop(0, imgs, image, 0)
        for g in range(imgs * height // 4):
            for a in range(4):
                for b in range(4):
                    q = 4 * a + b
                    for l in range(ch // 128):
                        off = (q % part_k) * ch + 128 * l
                        feat_f[q // part_k, g * group : (g + 1) * group, off : off + 128] = deep[
                            l, pl.ds((4 * g + a) * width + b, group, stride=4), :
                        ]
        feat[...] = feat_f[...].astype(bf16)
        sent = []
        for k in range(1, n):
            d = lax.rem(me + k, n)
            c = rc(feat.at[d], pieces.at[me], as_.at[k], ar.at[n - k], col=d)
            c.start()
            sent.append(c)
        terms[me] = jnp.dot(feat[me], p_ref[...], preferred_element_type=f32).astype(bf16)
        for k in range(1, n):
            d = lax.rem(me + k, n)
            rc(feat.at[d], pieces.at[d], as_.at[k], ar.at[k], col=d).wait_recv()
            terms[d] = jnp.dot(pieces[d], p_ref[...], preferred_element_type=f32).astype(bf16)
        far = [lax.rem(me + 2 * k, n) for k in range(zs)]
        mate_far = [lax.rem(mate + 2 * k, n) for k in range(zs)]
        order = sorted(range(1, zs), key=lambda k: -min(k, zs - k)) + [0]
        for k in order:
            c = rc(terms.at[mate_far[k]], near.at[k], s1.at[k], r1.at[k], col=mate)
            c.start()
            sent.append(c)
        for k in order:
            rc(terms.at[0], near.at[k], s1.at[k], r1.at[k], col=mate).wait_recv()
            tot = terms[far[k]].astype(f32) + near[k].astype(f32)
            if k:
                stage[k] = tot.astype(bf16)
                c = rc(stage.at[k], far_in.at[zs - k], s2.at[k], r2.at[zs - k], col=far[k])
                c.start()
                sent.append(c)
        for k in order[::-1][1:]:
            rc(stage.at[0], far_in.at[k], s2.at[k], r2.at[k], col=mate).wait_recv()
            tot = tot + far_in[k].astype(f32)
        o_ref[...] = tot
        for c in sent:
            c.wait_send()

    D = pltpu.SemaphoreType.DMA
    pad = -(-imgs * tall // 8) * 8
    return call(
        body,
        jax.ShapeDtypeStruct((tokens, model), f32),
        [first.reshape(imgs * height, width, ch), conv, patch_weight],
        [
            V((2, imgs, width, ch), bf16),
            V((2, imgs * height, ch), f32),
            V((2, imgs * height, ch), bf16),
            V((2, imgs * height, ch), bf16),
            V((4, imgs, ch), bf16),
            V((4, imgs, ch), bf16),
            V((2, pad, ch), f32),
            V((3, imgs * tall, width, ch), bf16),
            V((ch // 128, imgs * height * width, 128), f32),
            V((n, tokens, deep_k), f32),
            V((n, tokens, deep_k), bf16),
            V((n, tokens, deep_k), bf16),
            V((n, tokens, model), bf16),
        ]
        + [V((zs, tokens, model), bf16)] * 3
        + [D((8,)), D((8,)), D((n,)), D((n,))]
        + [D((zs,))] * 4,
        cid,
        "stem",
    )


def layer_norm(vectors, gain_vec):
    row_mean = jnp.mean(vectors, axis=-1, keepdims=True)
    center = vectors - row_mean
    spread = jnp.mean(center * center, axis=-1, keepdims=True)
    return center * lax.rsqrt(spread + 1e-06) * gain_vec


def on_device(
    images,
    stem_first,
    stem_conv,
    patch_weight,
    position,
    gain_attn,
    w_qkv,
    w_out,
    gain_mlp,
    w_up,
    w_down,
):
    first_map = jnp.einsum(
        "ikhw,kc->ihwc", images[0], stem_first, preferred_element_type=jnp.float32
    )
    stem_maps = jnp.maximum(first_map, 0.0).astype(jnp.bfloat16)
    embedded = stem_embed(stem_maps, stem_conv, patch_weight, 0)
    n = lax.axis_size("col")
    rows_n = lax.axis_size("row")
    model_width = patch_weight.shape[1]
    img_count, cols_here, rows_here = images.shape[1], images.shape[4] // 4, images.shape[3] // 4
    local_tokens = (
        embedded.reshape(img_count, rows_here, cols_here, model_width).transpose(0, 2, 1, 3)
        + position.astype(jnp.float32)[None]
    ).astype(jnp.bfloat16)
    arrived = swap_groups(local_tokens.reshape(rows_n, -1, model_width), 3)
    tokens_in = (
        arrived.reshape(rows_n, img_count // rows_n, cols_here, rows_here, model_width)
        .transpose(1, 2, 0, 3, 4)
        .reshape(-1, model_width)
    )
    residual = tokens_in.astype(jnp.float32)
    normed = layer_norm(residual, gain_attn).astype(jnp.bfloat16)
    projected = jnp.einsum(
        "td,kdh->kth",
        ag_line(normed, 4, 4).reshape(-1, model_width),
        w_qkv,
        preferred_element_type=jnp.float32,
    ).astype(jnp.bfloat16)
    token_count = projected.shape[1]
    local_heads = w_out.shape[0] // HD
    split_heads = projected.reshape(3, token_count, local_heads, HD).transpose(0, 2, 1, 3)
    key_heads = split_heads[1]
    value_heads = split_heads[2]
    block_rows = math.gcd(token_count, 512)
    query_blocks = (
        split_heads[0]
        .reshape(local_heads, token_count // block_rows, block_rows, HD)
        .transpose(1, 0, 2, 3)
    )

    def attend(query_block):
        scores = jnp.einsum(
            "hqd,hkd->hqk", query_block, key_heads, preferred_element_type=jnp.float32
        ) * HD ** (-0.5)
        row_peak = jnp.max(scores, axis=-1, keepdims=True)
        expo = jnp.exp(scores - row_peak)
        prob_rows = (expo / jnp.sum(expo, axis=-1, keepdims=True)).astype(jnp.bfloat16)
        return jnp.einsum(
            "hqk,hkd->hqd", prob_rows, value_heads, preferred_element_type=jnp.float32
        ).astype(jnp.bfloat16)

    attended = lax.map(attend, query_blocks)
    mixed_heads = attended.transpose(0, 2, 1, 3).reshape(token_count, local_heads * HD)
    row_slice = mixed_heads
    after = residual + rs_hier(
        jnp.dot(row_slice, w_out, preferred_element_type=jnp.float32)
        .astype(jnp.bfloat16)
        .reshape(n, -1, model_width),
        5,
    )
    normed_mlp = layer_norm(after, gain_mlp).astype(jnp.bfloat16)
    hidden = jax.nn.gelu(
        jnp.dot(
            ag_line(normed_mlp, 6, 4).reshape(-1, model_width),
            w_up,
            preferred_element_type=jnp.float32,
        ),
        approximate=True,
    ).astype(jnp.bfloat16)
    row_slice = hidden
    encoded = (
        after
        + rs_hier(
        jnp.dot(row_slice, w_down, preferred_element_type=jnp.float32)
        .astype(jnp.bfloat16)
        .reshape(n, -1, model_width),
        7,
    )
    ).astype(jnp.bfloat16)
    return encoded.reshape(1, 1, cols_here, -1, model_width)


def solution(mesh):
    placed = (
        P("section", None, None, "row", "col"),
        P(),
        P(),
        P("col", None),
        P("col", "row", None),
        P(),
        P(None, None, "col"),
        P("col", None),
        P(),
        P(None, "col"),
        P("col", None),
    )
    return jax.shard_map(
        on_device,
        mesh=mesh,
        in_specs=placed,
        out_specs=P("section", "row", "col", None, None),
        check_vma=False,
    )
```

```python
import functools
import math

import jax
import jax.numpy as jnp
from jax import lax
from jax.experimental import pallas as pl
from jax.experimental.pallas import tpu as pltpu
from jax.sharding import PartitionSpec as P

HD = 64
V = pltpu.VMEM


def call(body, out, ins, scratch, cid, name, far=()):
    return pl.pallas_call(
        body,
        out_shape=out,
        in_specs=[
            pl.BlockSpec(memory_space=pl.ANY if i in far else pltpu.VMEM) for i in range(len(ins))
        ],
        out_specs=pl.BlockSpec(memory_space=pltpu.VMEM),
        scratch_shapes=scratch,
        name=name,
        compiler_params=pltpu.CompilerParams(
            collective_id=cid, has_side_effects=True, vmem_limit_bytes=56 << 20
        ),
    )(*ins)


def rc(src, dst, ss, rs, **dev):
    return pltpu.make_async_remote_copy(src_ref=src, dst_ref=dst, send_sem=ss, recv_sem=rs, device_id=dev, device_id_type=pl.DeviceIdType.MESH)


def stem_embed(first, conv, patch_weight, cid):
    imgs, height, width, ch = first.shape
    rows_n, cols_n = lax.axis_size("row"), lax.axis_size("col")
    n, zs = cols_n, cols_n // 2
    tall, deep_k = height + 2, patch_weight.shape[0]
    model = patch_weight.shape[1]
    group = width // 4
    tokens = imgs * (height // 4) * group
    f32, bf16 = jnp.float32, jnp.bfloat16
    steps = [(a, b) for a in (-1, 0, 1) for b in (-1, 0, 1) if (a, b) != (0, 0)]

    def body(
        x_ref, w_hbm, p_hbm, o_ref,
        row_in, col_f, col_out, col_in, cor_out, cor_in, side, shifted, deep, feat_f, feat, pieces,
        terms, near, stage, far_in,
        hs, hr, as_, ar, s1, r1, s2, r2,
        w_ref, p_ref, fetch,
    ):
        get_conv = pltpu.make_async_copy(w_hbm, w_ref, fetch.at[0])
        get_conv.start()
        get_patch = pltpu.make_async_copy(p_hbm, p_ref, fetch.at[1])
        get_patch.start()
        r, me = lax.axis_index("row"), lax.axis_index("col")
        z, par = me // 2, lax.rem(me, 2)
        mate = me + 1 - 2 * par
        bar = pltpu.get_barrier_semaphore()

        def there(a, b):
            ok = jnp.int32(1)
            if a == -1:
                ok = ok * (r > 0).astype(jnp.int32)
            if a == 1:
                ok = ok * (r < rows_n - 1).astype(jnp.int32)
            if b == -1:
                ok = ok * (me > 0).astype(jnp.int32)
            if b == 1:
                ok = ok * (me < cols_n - 1).astype(jnp.int32)
            return ok

        def signal(dev):
            pl.semaphore_signal(bar, inc=1, device_id=dev, device_id_type=pl.DeviceIdType.MESH)

        have = [there(a, b) for a, b in steps]
        total = jnp.int32(n - 1)
        for k in range(1, n):
            signal({"col": lax.rem(me + k, n)})
        for (a, b), ok in zip(steps, have):
            if a != 0:
                total = total + ok
                pl.when(ok == 1)(lambda: signal({"row": r + a, "col": me + b}))

        def edges(i, carry):
            v = x_ref[i].astype(f32)
            col_f[0, pl.ds(i, 1), :] = v[:1]
            col_f[1, pl.ds(i, 1), :] = v[width - 1 :]
            return carry

        lax.fori_loop(0, imgs * height, edges, 0, unroll=4)
        col_out[...] = col_f[...].astype(bf16)
        for e in range(2):
            for f in range(2):
                for i in range(imgs):
                    at = i * height + (height - 1) * e
                    side[0, i : i + 1, :] = col_f[f, at : at + 1, :]
                cor_out[2 * e + f] = side[0, :imgs, :].astype(bf16)

        def route(a, b):
            if b == 0:
                e = (a + 1) // 2
                img = x_ref.reshape(imgs, height, width, ch)
                return img.at[:, (height - 1) * e], row_in.at[1 - e], row_in.at[e]
            if a == 0:
                f = (b + 1) // 2
                return col_out.at[f], col_in.at[1 - f], col_in.at[f]
            e, f = (a + 1) // 2, (b + 1) // 2
            return cor_out.at[2 * e + f], cor_in.at[3 - 2 * e - f], cor_in.at[2 * e + f]

        pl.semaphore_wait(bar, total)
        for j, ((a, b), ok) in enumerate(zip(steps, have)):
            src, there_ref, here_ref = route(a, b)

            @pl.when(ok == 1)
            def _():
                rc(src, there_ref, hs.at[j], hr.at[7 - j], row=r + a, col=me + b).start()

            @pl.when(ok == 0)
            def _():
                here_ref[...] = jnp.zeros_like(here_ref)

        for j, ((a, b), ok) in enumerate(zip(steps, have)):
            src, there_ref, here_ref = route(a, b)

            @pl.when(ok == 1)
            def _():
                c = rc(src, here_ref, hs.at[j], hr.at[j], row=r + a, col=me + b)
                c.wait_recv()
                c.wait_send()

        for f in range(2):
            for i in range(imgs):
                base = i * tall
                side[f, base + 1 : base + 1 + height, :] = col_in[
                    f, i * height : (i + 1) * height, :
                ].astype(f32)
            for e in range(2):
                got = cor_in[2 * e + f].astype(f32)
                for i in range(imgs):
                    at = i * tall + (tall - 1) * e
                    side[f, at : at + 1, :] = got[i : i + 1]
        place = lax.broadcasted_iota(jnp.int32, (width, ch), 0)

        def put(at, v):
            v = v.astype(f32)
            left = jnp.broadcast_to(side[0, pl.ds(at, 1), :], (width, ch))
            right = jnp.broadcast_to(side[1, pl.ds(at, 1), :], (width, ch))
            shifted[0, at] = jnp.where(place == 0, left, pltpu.roll(v, 1, 0)).astype(bf16)
            shifted[1, at] = v.astype(bf16)
            shifted[2, at] = jnp.where(
                place == width - 1, right, pltpu.roll(v, width - 1, 0)
            ).astype(bf16)

        for i in range(imgs):
            put(i * tall, row_in[0, i])
            put(i * tall + tall - 1, row_in[1, i])

        for i in range(imgs):

            def fill(h, carry):
                put(i * tall + 1 + h, x_ref[i * height + h])
                return carry

            lax.fori_loop(0, height, fill, 0, unroll=4)

        part_k = deep_k // ch
        get_conv.wait()

        def image(i, carry):
            acc = x_ref[pl.ds(i * height, height)].reshape(height * width, ch).astype(f32)
            for a in range(3):
                for b in range(3):
                    win = shifted[b, pl.ds(i * tall + a, height)].reshape(height * width, ch)
                    acc = acc + jnp.dot(win, w_ref[a, b], preferred_element_type=f32)
            acc = jnp.maximum(acc, 0.0).astype(bf16).astype(f32)
            pixels = pl.multiple_of(i * height * width, height * width)
            for l in range(ch // 128):
                deep[l, pl.ds(pixels, height * width), :] = acc[:, 128 * l : 128 * (l + 1)]
            return carry

        lax.fori_loop(0, imgs, image, 0)
        for g in range(imgs * height // 4):
            for a in range(4):
                for b in range(4):
                    q = 4 * a + b
                    for l in range(ch // 128):
                        off = (q % part_k) * ch + 128 * l
                        feat_f[q // part_k, g * group : (g + 1) * group, off : off + 128] = deep[
                            l, pl.ds((4 * g + a) * width + b, group, stride=4), :
                        ]
        feat[...] = feat_f[...].astype(bf16)
        sent = []
        for k in range(1, n):
            d = lax.rem(me + k, n)
            c = rc(feat.at[d], pieces.at[me], as_.at[k], ar.at[n - k], col=d)
            c.start()
            sent.append(c)
        get_patch.wait()
        terms[me] = jnp.dot(feat[me], p_ref[...], preferred_element_type=f32).astype(bf16)
        for k in range(1, n):
            d = lax.rem(me + k, n)
            rc(feat.at[d], pieces.at[d], as_.at[k], ar.at[k], col=d).wait_recv()
            terms[d] = jnp.dot(pieces[d], p_ref[...], preferred_element_type=f32).astype(bf16)
        far = [lax.rem(me + 2 * k, n) for k in range(zs)]
        mate_far = [lax.rem(mate + 2 * k, n) for k in range(zs)]
        order = sorted(range(1, zs), key=lambda k: -min(k, zs - k)) + [0]
        for k in order:
            c = rc(terms.at[mate_far[k]], near.at[k], s1.at[k], r1.at[k], col=mate)
            c.start()
            sent.append(c)
        for k in order:
            rc(terms.at[0], near.at[k], s1.at[k], r1.at[k], col=mate).wait_recv()
            tot = terms[far[k]].astype(f32) + near[k].astype(f32)
            if k:
                stage[k] = tot.astype(bf16)
                c = rc(stage.at[k], far_in.at[zs - k], s2.at[k], r2.at[zs - k], col=far[k])
                c.start()
                sent.append(c)
        for k in order[::-1][1:]:
            rc(stage.at[0], far_in.at[k], s2.at[k], r2.at[k], col=mate).wait_recv()
            tot = tot + far_in[k].astype(f32)
        o_ref[...] = tot
        for c in sent:
            c.wait_send()

    D = pltpu.SemaphoreType.DMA
    pad = -(-imgs * tall // 8) * 8
    return call(
        body,
        jax.ShapeDtypeStruct((tokens, model), f32),
        [first.reshape(imgs * height, width, ch), conv, patch_weight],
        [
            V((2, imgs, width, ch), bf16),
            V((2, imgs * height, ch), f32),
            V((2, imgs * height, ch), bf16),
            V((2, imgs * height, ch), bf16),
            V((4, imgs, ch), bf16),
            V((4, imgs, ch), bf16),
            V((2, pad, ch), f32),
            V((3, imgs * tall, width, ch), bf16),
            V((ch // 128, imgs * height * width, 128), f32),
            V((n, tokens, deep_k), f32),
            V((n, tokens, deep_k), bf16),
            V((n, tokens, deep_k), bf16),
            V((n, tokens, model), bf16),
        ]
        + [V((zs, tokens, model), bf16)] * 3
        + [D((8,)), D((8,)), D((n,)), D((n,))]
        + [D((zs,))] * 4
        + [V(conv.shape, bf16), V(patch_weight.shape, bf16), D((2,))],
        cid,
        "stem",
        far=(1, 2),
    )


def layer_norm(vectors, gain_vec):
    row_mean = jnp.mean(vectors, axis=-1, keepdims=True)
    center = vectors - row_mean
    spread = jnp.mean(center * center, axis=-1, keepdims=True)
    return center * lax.rsqrt(spread + 1e-06) * gain_vec


def layer(x, gain_attn, w_qkv, w_out, gain_mlp, w_up, w_down, cid):
    n, rows_n, secs = lax.axis_size("col"), lax.axis_size("row"), lax.axis_size("section")
    zs = n // 2
    width = x.shape[2]
    mine = x.shape[0] * x.shape[1]
    tokens = n * mine
    inner, hidden = w_out.shape[0], w_down.shape[0]
    heads = inner // HD
    chunks = 4
    piece = mine // chunks
    f32, bf16 = jnp.float32, jnp.bfloat16
    q_rows = math.gcd(tokens, 256)

    def body(
        x_ref, g1_ref, g2_ref, wq_hbm, wo_hbm, wu_hbm, wd_hbm, o_ref,
        arrived, res, all1, all2, qkv, att, terms1, terms2,
        near1, stage1, far1, near2, stage2, far2,
        wq, wo, wu, wd, fetch,
        xs, xr, su1, sd1, sm1, ru1, rd1, rm1, su2, sd2, sm2, ru2, rd2, rm2,
        a1, b1, c1, d1, a2, b2, c2, d2,
    ):
        gets = []
        for j, (src, dst) in enumerate(((wq_hbm, wq), (wo_hbm, wo), (wu_hbm, wu), (wd_hbm, wd))):
            gets.append(pltpu.make_async_copy(src, dst, fetch.at[j]))
            gets[-1].start()
        sec, row, me = lax.axis_index("section"), lax.axis_index("row"), lax.axis_index("col")
        z, par = me // 2, lax.rem(me, 2)
        mate = me + 1 - 2 * par
        far = [lax.rem(me + 2 * k, n) for k in range(zs)]
        chips = [lax.rem(z + k, zs) for k in range(zs)]
        order = sorted(range(1, zs), key=lambda k: -min(k, zs - k)) + [0]
        to, back = lax.rem(sec + 1, secs), lax.rem(sec + secs - 1, secs)
        bar = pltpu.get_barrier_semaphore()

        def signal(dev):
            pl.semaphore_signal(bar, inc=1, device_id=dev, device_id_type=pl.DeviceIdType.MESH)

        signal({"col": mate})
        for k in range(1, zs):
            signal({"col": far[k]})
        for k in range(rows_n):
            signal({"section": back, "row": lax.rem(row + k, rows_n)})
        pl.semaphore_wait(bar, zs + rows_n)
        sent = []
        for k in range(rows_n):
            d = lax.rem(row + k, rows_n)
            c = rc(
                x_ref.at[d], arrived.at[row], xs.at[k], xr.at[(rows_n - k) % rows_n],
                section=to, row=d,
            )
            c.start()
            sent.append(c)
        for k in range(rows_n):
            d = lax.rem(row + k, rows_n)
            rc(x_ref.at[d], arrived.at[d], xs.at[k], xr.at[k], section=to, row=d).wait_recv()
        res[...] = arrived[...].reshape(mine, width).astype(f32)
        lo, hi = z > 0, z < zs - 1

        def gather(full, su, sd, sm, ru, rd, rm):
            def part(blk, c):
                return full.at[blk, pl.ds(c * piece, piece)]

            def up(blk, c):
                return rc(
                    part(blk, c), part(blk, c), su.at[blk // 2, c], ru.at[blk // 2, c], col=me + 2
                )

            def down(blk, c):
                return rc(
                    part(blk, c), part(blk, c), sd.at[blk // 2, c], rd.at[blk // 2, c], col=me - 2
                )

            def side(blk, c):
                return rc(
                    part(blk, c), part(blk, c), sm.at[blk // 2, c], rm.at[blk // 2, c], col=mate
                )

            for c in range(chunks):
                pl.when(hi)(lambda: up(me, c).start())
                pl.when(lo)(lambda: down(me, c).start())
            for c in range(chunks):
                side(me, c).start()
            for k in range(1, zs):
                for c in range(chunks):

                    @pl.when(z - k >= 0)
                    def _():
                        b = me - 2 * k
                        up(b, c).wait_recv()
                        pl.when(hi)(lambda: up(b, c).start())
                        side(b, c).start()

                    @pl.when(z + k < zs)
                    def _():
                        b = me + 2 * k
                        down(b, c).wait_recv()
                        pl.when(lo)(lambda: down(b, c).start())
                        side(b, c).start()

            for j in range(zs):
                for c in range(chunks):
                    b = 2 * j + par
                    side(b, c).wait_send()
                    side(2 * j + 1 - par, c).wait_recv()

                    @pl.when(hi & (j <= z))
                    def _():
                        up(b, c).wait_send()

                    @pl.when(lo & (j >= z))
                    def _():
                        down(b, c).wait_send()

        def scatter_sum(make, terms, near, stage, far_in, s1, r1, s2, r2):
            for k in order:
                chip = chips[k]
                terms[pl.ds(2 * chip, 2)] = make(chip).astype(bf16).reshape(2, mine, width)
                c = rc(
                    terms.at[2 * chip + 1 - par], near.at[k], s1.at[k], r1.at[k], col=mate
                )
                c.start()
                sent.append(c)
            for k in order:
                rc(terms.at[0], near.at[k], s1.at[k], r1.at[k], col=mate).wait_recv()
                tot = terms[far[k]].astype(f32) + near[k].astype(f32)
                if k:
                    stage[k] = tot.astype(bf16)
                    c = rc(stage.at[k], far_in.at[zs - k], s2.at[k], r2.at[zs - k], col=far[k])
                    c.start()
                    sent.append(c)
            for k in order[::-1][1:]:
                rc(stage.at[0], far_in.at[k], s2.at[k], r2.at[k], col=mate).wait_recv()
                tot = tot + far_in[k].astype(f32)
            return tot

        all1[me] = layer_norm(res[...], g1_ref[...]).astype(bf16)
        gather(all1, su1, sd1, sm1, ru1, rd1, rm1)
        gets[0].wait()
        every = all1[...].reshape(tokens, width)
        for j in range(3):
            qkv[j] = jnp.dot(every, wq[j], preferred_element_type=f32).astype(bf16)

        def attend(i, carry):
            at = pl.multiple_of(i * q_rows, q_rows)
            outs = []
            for h in range(heads):
                q = qkv[0, pl.ds(at, q_rows), h * HD : (h + 1) * HD]
                keys = qkv[1, :, h * HD : (h + 1) * HD]
                vals = qkv[2, :, h * HD : (h + 1) * HD]
                scores = lax.dot_general(
                    q, keys, (((1,), (1,)), ((), ())), preferred_element_type=f32
                ) * HD ** (-0.5)
                expo = jnp.exp(scores - jnp.max(scores, axis=-1, keepdims=True))
                probs = expo * (1.0 / jnp.sum(expo, axis=-1, keepdims=True))
                outs.append(jnp.dot(probs.astype(bf16), vals, preferred_element_type=f32))
            joined = outs[0] if heads == 1 else jnp.concatenate(outs, axis=-1)
            att[pl.ds(at, q_rows), :] = joined.astype(bf16)
            return carry

        lax.fori_loop(0, tokens // q_rows, attend, 0)
        gets[1].wait()

        def mixed(chip):
            rows = pl.ds(pl.multiple_of(chip * 2 * mine, 2 * mine), 2 * mine)
            return jnp.dot(att[rows, :], wo[...], preferred_element_type=f32)

        res[...] = res[...] + scatter_sum(mixed, terms1, near1, stage1, far1, a1, b1, c1, d1)
        all2[me] = layer_norm(res[...], g2_ref[...]).astype(bf16)
        gather(all2, su2, sd2, sm2, ru2, rd2, rm2)
        gets[2].wait()
        gets[3].wait()

        def mlp(chip):
            block = all2[pl.ds(2 * chip, 2)].reshape(2 * mine, width)
            mid = jax.nn.gelu(
                jnp.dot(block, wu[...], preferred_element_type=f32), approximate=True
            ).astype(bf16)
            return jnp.dot(mid, wd[...], preferred_element_type=f32)

        total = scatter_sum(mlp, terms2, near2, stage2, far2, a2, b2, c2, d2)
        o_ref[...] = (res[...] + total).astype(bf16)
        for c in sent:
            c.wait_send()

    D = pltpu.SemaphoreType.DMA
    blocks = V((n, mine, width), bf16)
    quarter = V((zs, mine, width), bf16)
    return call(
        body,
        jax.ShapeDtypeStruct((mine, width), bf16),
        [x, gain_attn.reshape(1, -1), gain_mlp.reshape(1, -1), w_qkv, w_out, w_up, w_down],
        [
            V(x.shape, bf16),
            V((mine, width), f32),
            blocks,
            blocks,
            V((3, tokens, inner), bf16),
            V((tokens, inner), bf16),
            blocks,
            blocks,
        ]
        + [quarter] * 6
        + [V(w_qkv.shape, bf16), V(w_out.shape, bf16), V(w_up.shape, bf16), V(w_down.shape, bf16)]
        + [D((4,)), D((rows_n,)), D((rows_n,))]
        + [D((zs, chunks))] * 12
        + [D((zs,))] * 8,
        cid,
        "layer",
        far=(3, 4, 5, 6),
    )


def on_device(
    images,
    stem_first,
    stem_conv,
    patch_weight,
    position,
    gain_attn,
    w_qkv,
    w_out,
    gain_mlp,
    w_up,
    w_down,
):
    first_map = jnp.einsum(
        "ikhw,kc->ihwc", images[0], stem_first, preferred_element_type=jnp.float32
    )
    stem_maps = jnp.maximum(first_map, 0.0).astype(jnp.bfloat16)
    embedded = stem_embed(stem_maps, stem_conv, patch_weight, 0)
    n = lax.axis_size("col")
    rows_n = lax.axis_size("row")
    model_width = patch_weight.shape[1]
    img_count, cols_here, rows_here = images.shape[1], images.shape[4] // 4, images.shape[3] // 4
    local_tokens = (
        embedded.reshape(img_count, rows_here, cols_here, model_width).transpose(0, 2, 1, 3)
        + position.astype(jnp.float32)[None]
    ).astype(jnp.bfloat16)
    encoded = layer(
        local_tokens.reshape(rows_n, -1, model_width),
        gain_attn,
        w_qkv,
        w_out,
        gain_mlp,
        w_up,
        w_down,
        1,
    )
    return (
        encoded.reshape(rows_n, img_count // rows_n, cols_here, rows_here, model_width)
        .transpose(1, 2, 0, 3, 4)
        .reshape(1, img_count // rows_n, cols_here, -1, model_width)
    )


def solution(mesh):
    placed = (
        P("section", None, None, "row", "col"),
        P(),
        P(),
        P("col", None),
        P("col", "row", None),
        P(),
        P(None, None, "col"),
        P("col", None),
        P(),
        P(None, "col"),
        P("col", None),
    )
    return jax.shard_map(
        on_device,
        mesh=mesh,
        in_specs=placed,
        out_specs=P("section", "row", "col", None, None),
        check_vma=False,
    )
```

```python
import functools
import math

import jax
import jax.numpy as jnp
from jax import lax
from jax.experimental import pallas as pl
from jax.experimental.pallas import tpu as pltpu
from jax.sharding import PartitionSpec as P

HD = 64
V = pltpu.VMEM


def call(body, out, ins, scratch, cid, name, far=()):
    return pl.pallas_call(
        body,
        out_shape=out,
        in_specs=[
            pl.BlockSpec(memory_space=pl.ANY if i in far else pltpu.VMEM) for i in range(len(ins))
        ],
        out_specs=pl.BlockSpec(memory_space=pltpu.VMEM),
        scratch_shapes=scratch,
        name=name,
        compiler_params=pltpu.CompilerParams(
            collective_id=cid, has_side_effects=True, vmem_limit_bytes=56 << 20
        ),
    )(*ins)


def rc(src, dst, ss, rs, **dev):
    return pltpu.make_async_remote_copy(src_ref=src, dst_ref=dst, send_sem=ss, recv_sem=rs, device_id=dev, device_id_type=pl.DeviceIdType.MESH)


def stem_embed(first, conv, patch_weight, cid):
    imgs, height, width, ch = first.shape
    rows_n, cols_n = lax.axis_size("row"), lax.axis_size("col")
    n, zs = cols_n, cols_n // 2
    tall, deep_k = height + 2, patch_weight.shape[0]
    model = patch_weight.shape[1]
    group = width // 4
    tokens = imgs * (height // 4) * group
    halves = 2 if imgs % 2 == 0 else 1
    some = tokens // halves
    f32, bf16 = jnp.float32, jnp.bfloat16
    steps = [(a, b) for a in (-1, 0, 1) for b in (-1, 0, 1) if (a, b) != (0, 0)]

    def body(
        x_ref, w_hbm, p_hbm, o_ref,
        row_in, col_f, col_out, col_in, cor_out, cor_in, side, shifted, deep, feat_f, feat, pieces,
        terms, near, stage, far_in,
        hs, hr, as_, ar, s1, r1, s2, r2,
        w_ref, p_ref, fetch,
    ):
        get_conv = pltpu.make_async_copy(w_hbm, w_ref, fetch.at[0])
        get_conv.start()
        get_patch = pltpu.make_async_copy(p_hbm, p_ref, fetch.at[1])
        get_patch.start()
        r, me = lax.axis_index("row"), lax.axis_index("col")
        z, par = me // 2, lax.rem(me, 2)
        mate = me + 1 - 2 * par
        bar = pltpu.get_barrier_semaphore()

        def there(a, b):
            ok = jnp.int32(1)
            if a == -1:
                ok = ok * (r > 0).astype(jnp.int32)
            if a == 1:
                ok = ok * (r < rows_n - 1).astype(jnp.int32)
            if b == -1:
                ok = ok * (me > 0).astype(jnp.int32)
            if b == 1:
                ok = ok * (me < cols_n - 1).astype(jnp.int32)
            return ok

        def signal(dev):
            pl.semaphore_signal(bar, inc=1, device_id=dev, device_id_type=pl.DeviceIdType.MESH)

        have = [there(a, b) for a, b in steps]
        total = jnp.int32(n - 1)
        for k in range(1, n):
            signal({"col": lax.rem(me + k, n)})
        for (a, b), ok in zip(steps, have):
            if a != 0:
                total = total + ok
                pl.when(ok == 1)(lambda: signal({"row": r + a, "col": me + b}))

        def edges(i, carry):
            v = x_ref[i].astype(f32)
            col_f[0, pl.ds(i, 1), :] = v[:1]
            col_f[1, pl.ds(i, 1), :] = v[width - 1 :]
            return carry

        lax.fori_loop(0, imgs * height, edges, 0, unroll=4)
        col_out[...] = col_f[...].astype(bf16)
        for e in range(2):
            for f in range(2):
                for i in range(imgs):
                    at = i * height + (height - 1) * e
                    side[0, i : i + 1, :] = col_f[f, at : at + 1, :]
                cor_out[2 * e + f] = side[0, :imgs, :].astype(bf16)

        def route(a, b):
            if b == 0:
                e = (a + 1) // 2
                img = x_ref.reshape(imgs, height, width, ch)
                return img.at[:, (height - 1) * e], row_in.at[1 - e], row_in.at[e]
            if a == 0:
                f = (b + 1) // 2
                return col_out.at[f], col_in.at[1 - f], col_in.at[f]
            e, f = (a + 1) // 2, (b + 1) // 2
            return cor_out.at[2 * e + f], cor_in.at[3 - 2 * e - f], cor_in.at[2 * e + f]

        pl.semaphore_wait(bar, total)
        for j, ((a, b), ok) in enumerate(zip(steps, have)):
            src, there_ref, here_ref = route(a, b)

            @pl.when(ok == 1)
            def _():
                rc(src, there_ref, hs.at[j], hr.at[7 - j], row=r + a, col=me + b).start()

            @pl.when(ok == 0)
            def _():
                here_ref[...] = jnp.zeros_like(here_ref)

        for j, ((a, b), ok) in enumerate(zip(steps, have)):
            src, there_ref, here_ref = route(a, b)

            @pl.when(ok == 1)
            def _():
                c = rc(src, here_ref, hs.at[j], hr.at[j], row=r + a, col=me + b)
                c.wait_recv()
                c.wait_send()

        for f in range(2):
            for i in range(imgs):
                base = i * tall
                side[f, base + 1 : base + 1 + height, :] = col_in[
                    f, i * height : (i + 1) * height, :
                ].astype(f32)
            for e in range(2):
                got = cor_in[2 * e + f].astype(f32)
                for i in range(imgs):
                    at = i * tall + (tall - 1) * e
                    side[f, at : at + 1, :] = got[i : i + 1]
        place = lax.broadcasted_iota(jnp.int32, (width, ch), 0)

        def put(at, v):
            v = v.astype(f32)
            left = jnp.broadcast_to(side[0, pl.ds(at, 1), :], (width, ch))
            right = jnp.broadcast_to(side[1, pl.ds(at, 1), :], (width, ch))
            shifted[0, at] = jnp.where(place == 0, left, pltpu.roll(v, 1, 0)).astype(bf16)
            shifted[1, at] = v.astype(bf16)
            shifted[2, at] = jnp.where(
                place == width - 1, right, pltpu.roll(v, width - 1, 0)
            ).astype(bf16)

        for i in range(imgs):
            put(i * tall, row_in[0, i])
            put(i * tall + tall - 1, row_in[1, i])

        for i in range(imgs):

            def fill(h, carry):
                put(i * tall + 1 + h, x_ref[i * height + h])
                return carry

            lax.fori_loop(0, height, fill, 0, unroll=4)

        part_k = deep_k // ch
        get_conv.wait()

        def image(i, carry):
            acc = x_ref[pl.ds(i * height, height)].reshape(height * width, ch).astype(f32)
            for a in range(3):
                for b in range(3):
                    win = shifted[b, pl.ds(i * tall + a, height)].reshape(height * width, ch)
                    acc = acc + jnp.dot(win, w_ref[a, b], preferred_element_type=f32)
            acc = jnp.maximum(acc, 0.0).astype(bf16).astype(f32)
            pixels = pl.multiple_of(i * height * width, height * width)
            for l in range(ch // 128):
                deep[l, pl.ds(pixels, height * width), :] = acc[:, 128 * l : 128 * (l + 1)]
            return carry

        far = [lax.rem(me + 2 * k, n) for k in range(zs)]
        mate_far = [lax.rem(mate + 2 * k, n) for k in range(zs)]
        order = sorted(range(1, zs), key=lambda k: -min(k, zs - k)) + [0]
        reach = sorted(range(1, n), key=lambda k: -min(k, n - k))
        sent = []
        for half in range(halves):
            lax.fori_loop(half * imgs // halves, (half + 1) * imgs // halves, image, 0)
            bands = imgs * height // 4 // halves
            for g in range(half * bands, (half + 1) * bands):
                for a in range(4):
                    for b in range(4):
                        q = 4 * a + b
                        for l in range(ch // 128):
                            off = (q % part_k) * ch + 128 * l
                            feat_f[q // part_k, g * group : (g + 1) * group, off : off + 128] = (
                                deep[l, pl.ds((4 * g + a) * width + b, group, stride=4), :]
                            )
            rows = slice(half * some, (half + 1) * some)
            feat[half] = feat_f[:, rows, :].astype(bf16)
            for k in reach:
                d = lax.rem(me + k, n)
                c = rc(
                    feat.at[half, d], pieces.at[half, me], as_.at[half, k], ar.at[half, n - k],
                    col=d,
                )
                c.start()
                sent.append(c)
            pieces[half, me] = feat[half, me]
        get_patch.wait()
        for half in range(halves):
            rows = slice(half * some, (half + 1) * some)

            def combine(k):
                rc(
                    terms.at[half, 0], near.at[half, k], s1.at[half, k], r1.at[half, k], col=mate
                ).wait_recv()
                tot = terms[half, far[k]].astype(f32) + near[half, k].astype(f32)
                if k:
                    stage[half, k] = tot.astype(bf16)
                    c = rc(
                        stage.at[half, k], far_in.at[half, zs - k], s2.at[half, k],
                        r2.at[half, zs - k], col=far[k],
                    )
                    c.start()
                    sent.append(c)
                else:
                    o_ref[rows, :] = tot

            for j, k in enumerate(order):
                for d, off in ((far[k], 2 * k), (mate_far[k], None)):
                    if off is None:
                        off = lax.rem(d - me + n, n)
                    if k or d is not far[k]:
                        rc(
                            feat.at[half, 0], pieces.at[half, d], as_.at[half, off],
                            ar.at[half, off], col=d,
                        ).wait_recv()
                chip = lax.rem(z + k, zs)
                both = pieces[half, pl.ds(2 * chip, 2)].reshape(2 * some, deep_k)
                terms[half, pl.ds(2 * chip, 2)] = (
                    jnp.dot(both, p_ref[...], preferred_element_type=f32)
                    .astype(bf16)
                    .reshape(2, some, model)
                )
                c = rc(
                    terms.at[half, mate_far[k]], near.at[half, k], s1.at[half, k], r1.at[half, k],
                    col=mate,
                )
                c.start()
                sent.append(c)
                if j:
                    combine(order[j - 1])
            combine(order[-1])
        for half in range(halves):
            rows = slice(half * some, (half + 1) * some)
            tot = o_ref[rows, :]
            for k in order[::-1][1:]:
                rc(
                    stage.at[half, 0], far_in.at[half, k], s2.at[half, k], r2.at[half, k], col=mate
                ).wait_recv()
                tot = tot + far_in[half, k].astype(f32)
            o_ref[rows, :] = tot
        for c in sent:
            c.wait_send()

    D = pltpu.SemaphoreType.DMA
    pad = -(-imgs * tall // 8) * 8
    return call(
        body,
        jax.ShapeDtypeStruct((tokens, model), f32),
        [first.reshape(imgs * height, width, ch), conv, patch_weight],
        [
            V((2, imgs, width, ch), bf16),
            V((2, imgs * height, ch), f32),
            V((2, imgs * height, ch), bf16),
            V((2, imgs * height, ch), bf16),
            V((4, imgs, ch), bf16),
            V((4, imgs, ch), bf16),
            V((2, pad, ch), f32),
            V((3, imgs * tall, width, ch), bf16),
            V((ch // 128, imgs * height * width, 128), f32),
            V((n, tokens, deep_k), f32),
            V((halves, n, some, deep_k), bf16),
            V((halves, n, some, deep_k), bf16),
            V((halves, n, some, model), bf16),
        ]
        + [V((halves, zs, some, model), bf16)] * 3
        + [D((8,)), D((8,)), D((halves, n)), D((halves, n))]
        + [D((halves, zs))] * 4
        + [V(conv.shape, bf16), V(patch_weight.shape, bf16), D((2,))],
        cid,
        "stem",
        far=(1, 2),
    )


def layer_norm(vectors, gain_vec):
    row_mean = jnp.mean(vectors, axis=-1, keepdims=True)
    center = vectors - row_mean
    spread = jnp.mean(center * center, axis=-1, keepdims=True)
    return center * lax.rsqrt(spread + 1e-06) * gain_vec


def layer(x, gain_attn, w_qkv, w_out, gain_mlp, w_up, w_down, cid):
    n, rows_n, secs = lax.axis_size("col"), lax.axis_size("row"), lax.axis_size("section")
    zs = n // 2
    width = x.shape[2]
    mine = x.shape[0] * x.shape[1]
    tokens = n * mine
    inner, hidden = w_out.shape[0], w_down.shape[0]
    heads = inner // HD
    chunks = 4
    piece = mine // chunks
    f32, bf16 = jnp.float32, jnp.bfloat16
    q_rows = math.gcd(tokens, 256)

    def body(
        x_ref, g1_ref, g2_ref, wq_hbm, wo_hbm, wu_hbm, wd_hbm, o_ref,
        arrived, res, all1, all2, qkv, att, terms1, terms2,
        near1, stage1, far1, near2, stage2, far2,
        wq, wo, wu, wd, fetch,
        xs, xr, su1, sd1, sm1, ru1, rd1, rm1, su2, sd2, sm2, ru2, rd2, rm2,
        a1, b1, c1, d1, a2, b2, c2, d2,
    ):
        gets = []
        for j, (src, dst) in enumerate(((wq_hbm, wq), (wo_hbm, wo), (wu_hbm, wu), (wd_hbm, wd))):
            gets.append(pltpu.make_async_copy(src, dst, fetch.at[j]))
            gets[-1].start()
        sec, row, me = lax.axis_index("section"), lax.axis_index("row"), lax.axis_index("col")
        z, par = me // 2, lax.rem(me, 2)
        mate = me + 1 - 2 * par
        far = [lax.rem(me + 2 * k, n) for k in range(zs)]
        chips = [lax.rem(z + k, zs) for k in range(zs)]
        order = sorted(range(1, zs), key=lambda k: -min(k, zs - k)) + [0]
        to, back = lax.rem(sec + 1, secs), lax.rem(sec + secs - 1, secs)
        bar = pltpu.get_barrier_semaphore()

        def signal(dev):
            pl.semaphore_signal(bar, inc=1, device_id=dev, device_id_type=pl.DeviceIdType.MESH)

        signal({"col": mate})
        for k in range(1, zs):
            signal({"col": far[k]})
        for k in range(rows_n):
            signal({"section": back, "row": lax.rem(row + k, rows_n)})
        pl.semaphore_wait(bar, zs + rows_n)
        sent = []
        for k in range(rows_n):
            d = lax.rem(row + k, rows_n)
            c = rc(
                x_ref.at[d], arrived.at[row], xs.at[k], xr.at[(rows_n - k) % rows_n],
                section=to, row=d,
            )
            c.start()
            sent.append(c)
        for k in range(rows_n):
            d = lax.rem(row + k, rows_n)
            rc(x_ref.at[d], arrived.at[d], xs.at[k], xr.at[k], section=to, row=d).wait_recv()
        res[...] = arrived[...].reshape(mine, width).astype(f32)
        lo, hi = z > 0, z < zs - 1

        def gather(full, su, sd, sm, ru, rd, rm):
            def part(blk, c):
                return full.at[blk, pl.ds(c * piece, piece)]

            def up(blk, c):
                return rc(
                    part(blk, c), part(blk, c), su.at[blk // 2, c], ru.at[blk // 2, c], col=me + 2
                )

            def down(blk, c):
                return rc(
                    part(blk, c), part(blk, c), sd.at[blk // 2, c], rd.at[blk // 2, c], col=me - 2
                )

            def side(blk, c):
                return rc(
                    part(blk, c), part(blk, c), sm.at[blk // 2, c], rm.at[blk // 2, c], col=mate
                )

            for c in range(chunks):
                pl.when(hi)(lambda: up(me, c).start())
                pl.when(lo)(lambda: down(me, c).start())
            for c in range(chunks):
                side(me, c).start()
            for k in range(1, zs):
                for c in range(chunks):

                    @pl.when(z - k >= 0)
                    def _():
                        b = me - 2 * k
                        up(b, c).wait_recv()
                        pl.when(hi)(lambda: up(b, c).start())
                        side(b, c).start()

                    @pl.when(z + k < zs)
                    def _():
                        b = me + 2 * k
                        down(b, c).wait_recv()
                        pl.when(lo)(lambda: down(b, c).start())
                        side(b, c).start()

            for j in range(zs):
                for c in range(chunks):
                    b = 2 * j + par
                    side(b, c).wait_send()
                    side(2 * j + 1 - par, c).wait_recv()

                    @pl.when(hi & (j <= z))
                    def _():
                        up(b, c).wait_send()

                    @pl.when(lo & (j >= z))
                    def _():
                        down(b, c).wait_send()

        def scatter_sum(make, terms, near, stage, far_in, s1, r1, s2, r2):
            def combine(k):
                rc(terms.at[0], near.at[k], s1.at[k], r1.at[k], col=mate).wait_recv()
                tot = terms[far[k]].astype(f32) + near[k].astype(f32)
                if k:
                    stage[k] = tot.astype(bf16)
                    c = rc(stage.at[k], far_in.at[zs - k], s2.at[k], r2.at[zs - k], col=far[k])
                    c.start()
                    sent.append(c)
                return tot

            for j, k in enumerate(order):
                chip = chips[k]
                terms[pl.ds(2 * chip, 2)] = make(chip).astype(bf16).reshape(2, mine, width)
                c = rc(
                    terms.at[2 * chip + 1 - par], near.at[k], s1.at[k], r1.at[k], col=mate
                )
                c.start()
                sent.append(c)
                if j:
                    combine(order[j - 1])
            tot = combine(order[-1])
            for k in order[::-1][1:]:
                rc(stage.at[0], far_in.at[k], s2.at[k], r2.at[k], col=mate).wait_recv()
                tot = tot + far_in[k].astype(f32)
            return tot

        all1[me] = layer_norm(res[...], g1_ref[...]).astype(bf16)
        gather(all1, su1, sd1, sm1, ru1, rd1, rm1)
        gets[0].wait()
        every = all1[...].reshape(tokens, width)
        for j in range(3):
            qkv[j] = jnp.dot(every, wq[j], preferred_element_type=f32).astype(bf16)

        def attend(i, carry):
            at = pl.multiple_of(i * q_rows, q_rows)
            outs = []
            for h in range(heads):
                q = qkv[0, pl.ds(at, q_rows), h * HD : (h + 1) * HD]
                keys = qkv[1, :, h * HD : (h + 1) * HD]
                vals = qkv[2, :, h * HD : (h + 1) * HD]
                scores = lax.dot_general(
                    q, keys, (((1,), (1,)), ((), ())), preferred_element_type=f32
                ) * HD ** (-0.5)
                expo = jnp.exp(scores - jnp.max(scores, axis=-1, keepdims=True))
                probs = expo * (1.0 / jnp.sum(expo, axis=-1, keepdims=True))
                outs.append(jnp.dot(probs.astype(bf16), vals, preferred_element_type=f32))
            joined = outs[0] if heads == 1 else jnp.concatenate(outs, axis=-1)
            att[pl.ds(at, q_rows), :] = joined.astype(bf16)
            return carry

        lax.fori_loop(0, tokens // q_rows, attend, 0)
        gets[1].wait()

        def mixed(chip):
            rows = pl.ds(pl.multiple_of(chip * 2 * mine, 2 * mine), 2 * mine)
            return jnp.dot(att[rows, :], wo[...], preferred_element_type=f32)

        res[...] = res[...] + scatter_sum(mixed, terms1, near1, stage1, far1, a1, b1, c1, d1)
        all2[me] = layer_norm(res[...], g2_ref[...]).astype(bf16)
        gather(all2, su2, sd2, sm2, ru2, rd2, rm2)
        gets[2].wait()
        gets[3].wait()

        def mlp(chip):
            block = all2[pl.ds(2 * chip, 2)].reshape(2 * mine, width)
            mid = jax.nn.gelu(
                jnp.dot(block, wu[...], preferred_element_type=f32), approximate=True
            ).astype(bf16)
            return jnp.dot(mid, wd[...], preferred_element_type=f32)

        total = scatter_sum(mlp, terms2, near2, stage2, far2, a2, b2, c2, d2)
        o_ref[...] = (res[...] + total).astype(bf16)
        for c in sent:
            c.wait_send()

    D = pltpu.SemaphoreType.DMA
    blocks = V((n, mine, width), bf16)
    quarter = V((zs, mine, width), bf16)
    return call(
        body,
        jax.ShapeDtypeStruct((mine, width), bf16),
        [x, gain_attn.reshape(1, -1), gain_mlp.reshape(1, -1), w_qkv, w_out, w_up, w_down],
        [
            V(x.shape, bf16),
            V((mine, width), f32),
            blocks,
            blocks,
            V((3, tokens, inner), bf16),
            V((tokens, inner), bf16),
            blocks,
            blocks,
        ]
        + [quarter] * 6
        + [V(w_qkv.shape, bf16), V(w_out.shape, bf16), V(w_up.shape, bf16), V(w_down.shape, bf16)]
        + [D((4,)), D((rows_n,)), D((rows_n,))]
        + [D((zs, chunks))] * 12
        + [D((zs,))] * 8,
        cid,
        "layer",
        far=(3, 4, 5, 6),
    )


def on_device(
    images,
    stem_first,
    stem_conv,
    patch_weight,
    position,
    gain_attn,
    w_qkv,
    w_out,
    gain_mlp,
    w_up,
    w_down,
):
    first_map = jnp.einsum(
        "ikhw,kc->ihwc", images[0], stem_first, preferred_element_type=jnp.float32
    )
    stem_maps = jnp.maximum(first_map, 0.0).astype(jnp.bfloat16)
    embedded = stem_embed(stem_maps, stem_conv, patch_weight, 0)
    n = lax.axis_size("col")
    rows_n = lax.axis_size("row")
    model_width = patch_weight.shape[1]
    img_count, cols_here, rows_here = images.shape[1], images.shape[4] // 4, images.shape[3] // 4
    local_tokens = (
        embedded.reshape(img_count, rows_here, cols_here, model_width).transpose(0, 2, 1, 3)
        + position.astype(jnp.float32)[None]
    ).astype(jnp.bfloat16)
    encoded = layer(
        local_tokens.reshape(rows_n, -1, model_width),
        gain_attn,
        w_qkv,
        w_out,
        gain_mlp,
        w_up,
        w_down,
        1,
    )
    return (
        encoded.reshape(rows_n, img_count // rows_n, cols_here, rows_here, model_width)
        .transpose(1, 2, 0, 3, 4)
        .reshape(1, img_count // rows_n, cols_here, -1, model_width)
    )


def solution(mesh):
    placed = (
        P("section", None, None, "row", "col"),
        P(),
        P(),
        P("col", None),
        P("col", "row", None),
        P(),
        P(None, None, "col"),
        P("col", None),
        P(),
        P(None, "col"),
        P("col", None),
    )
    return jax.shard_map(
        on_device,
        mesh=mesh,
        in_specs=placed,
        out_specs=P("section", "row", "col", None, None),
        check_vma=False,
    )
```

```python
import functools
import math

import jax
import jax.numpy as jnp
from jax import lax
from jax.experimental import pallas as pl
from jax.experimental.pallas import tpu as pltpu
from jax.sharding import PartitionSpec as P

HD = 64
V = pltpu.VMEM


def call(body, out, ins, scratch, cid, name, far=()):
    return pl.pallas_call(
        body,
        out_shape=out,
        in_specs=[
            pl.BlockSpec(memory_space=pl.ANY if i in far else pltpu.VMEM) for i in range(len(ins))
        ],
        out_specs=pl.BlockSpec(memory_space=pltpu.VMEM),
        scratch_shapes=scratch,
        name=name,
        compiler_params=pltpu.CompilerParams(
            collective_id=cid, has_side_effects=True, vmem_limit_bytes=56 << 20
        ),
    )(*ins)


def rc(src, dst, ss, rs, **dev):
    return pltpu.make_async_remote_copy(src_ref=src, dst_ref=dst, send_sem=ss, recv_sem=rs, device_id=dev, device_id_type=pl.DeviceIdType.MESH)


def stem_embed(first, conv, patch_weight, place_rows, cid):
    imgs, height, width, ch = first.shape
    rows_n, cols_n = lax.axis_size("row"), lax.axis_size("col")
    n, zs = cols_n, cols_n // 2
    tall, deep_k = height + 2, patch_weight.shape[0]
    model = patch_weight.shape[1]
    group = width // 4
    tokens = imgs * (height // 4) * group
    halves = 2 if imgs % 2 == 0 else 1
    some = tokens // halves
    f32, bf16 = jnp.float32, jnp.bfloat16
    steps = [(a, b) for a in (-1, 0, 1) for b in (-1, 0, 1) if (a, b) != (0, 0)]

    def body(
        x_ref, w_hbm, p_hbm, pos_ref, o_ref,
        sums, row_in, col_f, col_out, col_in, cor_out, cor_in, side, shifted, deep, feat_f, feat, pieces,
        terms, near, stage, far_in,
        hs, hr, as_, ar, s1, r1, s2, r2,
        w_ref, p_ref, fetch,
    ):
        get_conv = pltpu.make_async_copy(w_hbm, w_ref, fetch.at[0])
        get_conv.start()
        get_patch = pltpu.make_async_copy(p_hbm, p_ref, fetch.at[1])
        get_patch.start()
        r, me = lax.axis_index("row"), lax.axis_index("col")
        z, par = me // 2, lax.rem(me, 2)
        mate = me + 1 - 2 * par
        bar = pltpu.get_barrier_semaphore()

        def there(a, b):
            ok = jnp.int32(1)
            if a == -1:
                ok = ok * (r > 0).astype(jnp.int32)
            if a == 1:
                ok = ok * (r < rows_n - 1).astype(jnp.int32)
            if b == -1:
                ok = ok * (me > 0).astype(jnp.int32)
            if b == 1:
                ok = ok * (me < cols_n - 1).astype(jnp.int32)
            return ok

        def signal(dev):
            pl.semaphore_signal(bar, inc=1, device_id=dev, device_id_type=pl.DeviceIdType.MESH)

        have = [there(a, b) for a, b in steps]
        total = jnp.int32(n - 1)
        for k in range(1, n):
            signal({"col": lax.rem(me + k, n)})
        for (a, b), ok in zip(steps, have):
            if a != 0:
                total = total + ok
                pl.when(ok == 1)(lambda: signal({"row": r + a, "col": me + b}))

        def edges(i, carry):
            v = x_ref[i].astype(f32)
            col_f[0, pl.ds(i, 1), :] = v[:1]
            col_f[1, pl.ds(i, 1), :] = v[width - 1 :]
            return carry

        lax.fori_loop(0, imgs * height, edges, 0, unroll=4)
        col_out[...] = col_f[...].astype(bf16)
        for e in range(2):
            for f in range(2):
                for i in range(imgs):
                    at = i * height + (height - 1) * e
                    side[0, i : i + 1, :] = col_f[f, at : at + 1, :]
                cor_out[2 * e + f] = side[0, :imgs, :].astype(bf16)

        def route(a, b):
            if b == 0:
                e = (a + 1) // 2
                img = x_ref.reshape(imgs, height, width, ch)
                return img.at[:, (height - 1) * e], row_in.at[1 - e], row_in.at[e]
            if a == 0:
                f = (b + 1) // 2
                return col_out.at[f], col_in.at[1 - f], col_in.at[f]
            e, f = (a + 1) // 2, (b + 1) // 2
            return cor_out.at[2 * e + f], cor_in.at[3 - 2 * e - f], cor_in.at[2 * e + f]

        pl.semaphore_wait(bar, total)
        for j, ((a, b), ok) in enumerate(zip(steps, have)):
            src, there_ref, here_ref = route(a, b)

            @pl.when(ok == 1)
            def _():
                rc(src, there_ref, hs.at[j], hr.at[7 - j], row=r + a, col=me + b).start()

            @pl.when(ok == 0)
            def _():
                here_ref[...] = jnp.zeros_like(here_ref)

        for j, ((a, b), ok) in enumerate(zip(steps, have)):
            src, there_ref, here_ref = route(a, b)

            @pl.when(ok == 1)
            def _():
                c = rc(src, here_ref, hs.at[j], hr.at[j], row=r + a, col=me + b)
                c.wait_recv()
                c.wait_send()

        for f in range(2):
            for i in range(imgs):
                base = i * tall
                side[f, base + 1 : base + 1 + height, :] = col_in[
                    f, i * height : (i + 1) * height, :
                ].astype(f32)
            for e in range(2):
                got = cor_in[2 * e + f].astype(f32)
                for i in range(imgs):
                    at = i * tall + (tall - 1) * e
                    side[f, at : at + 1, :] = got[i : i + 1]
        place = lax.broadcasted_iota(jnp.int32, (width, ch), 0)

        def put(at, v):
            v = v.astype(f32)
            left = jnp.broadcast_to(side[0, pl.ds(at, 1), :], (width, ch))
            right = jnp.broadcast_to(side[1, pl.ds(at, 1), :], (width, ch))
            shifted[0, at] = jnp.where(place == 0, left, pltpu.roll(v, 1, 0)).astype(bf16)
            shifted[1, at] = v.astype(bf16)
            shifted[2, at] = jnp.where(
                place == width - 1, right, pltpu.roll(v, width - 1, 0)
            ).astype(bf16)

        for i in range(imgs):
            put(i * tall, row_in[0, i])
            put(i * tall + tall - 1, row_in[1, i])

        for i in range(imgs):

            def fill(h, carry):
                put(i * tall + 1 + h, x_ref[i * height + h])
                return carry

            lax.fori_loop(0, height, fill, 0, unroll=4)

        part_k = deep_k // ch
        get_conv.wait()

        def image(i, carry):
            acc = x_ref[pl.ds(i * height, height)].reshape(height * width, ch).astype(f32)
            for a in range(3):
                for b in range(3):
                    win = shifted[b, pl.ds(i * tall + a, height)].reshape(height * width, ch)
                    acc = acc + jnp.dot(win, w_ref[a, b], preferred_element_type=f32)
            acc = jnp.maximum(acc, 0.0).astype(bf16).astype(f32)
            pixels = pl.multiple_of(i * height * width, height * width)
            for l in range(ch // 128):
                deep[l, pl.ds(pixels, height * width), :] = acc[:, 128 * l : 128 * (l + 1)]
            return carry

        far = [lax.rem(me + 2 * k, n) for k in range(zs)]
        mate_far = [lax.rem(mate + 2 * k, n) for k in range(zs)]
        order = sorted(range(1, zs), key=lambda k: -min(k, zs - k)) + [0]
        reach = sorted(range(1, n), key=lambda k: -min(k, n - k))
        sent = []
        for half in range(halves):
            lax.fori_loop(half * imgs // halves, (half + 1) * imgs // halves, image, 0)
            bands = imgs * height // 4 // halves
            for g in range(half * bands, (half + 1) * bands):
                for a in range(4):
                    for b in range(4):
                        q = 4 * a + b
                        for l in range(ch // 128):
                            off = (q % part_k) * ch + 128 * l
                            feat_f[q // part_k, g * group : (g + 1) * group, off : off + 128] = (
                                deep[l, pl.ds((4 * g + a) * width + b, group, stride=4), :]
                            )
            rows = slice(half * some, (half + 1) * some)
            feat[half] = feat_f[:, rows, :].astype(bf16)
            for k in reach:
                d = lax.rem(me + k, n)
                c = rc(
                    feat.at[half, d], pieces.at[half, me], as_.at[half, k], ar.at[half, n - k],
                    col=d,
                )
                c.start()
                sent.append(c)
            pieces[half, me] = feat[half, me]
        get_patch.wait()
        for half in range(halves):
            rows = slice(half * some, (half + 1) * some)

            def combine(k):
                rc(
                    terms.at[half, 0], near.at[half, k], s1.at[half, k], r1.at[half, k], col=mate
                ).wait_recv()
                tot = terms[half, far[k]].astype(f32) + near[half, k].astype(f32)
                if k:
                    stage[half, k] = tot.astype(bf16)
                    c = rc(
                        stage.at[half, k], far_in.at[half, zs - k], s2.at[half, k],
                        r2.at[half, zs - k], col=far[k],
                    )
                    c.start()
                    sent.append(c)
                else:
                    sums[rows, :] = tot

            for j, k in enumerate(order):
                for d, off in ((far[k], 2 * k), (mate_far[k], None)):
                    if off is None:
                        off = lax.rem(d - me + n, n)
                    if k or d is not far[k]:
                        rc(
                            feat.at[half, 0], pieces.at[half, d], as_.at[half, off],
                            ar.at[half, off], col=d,
                        ).wait_recv()
                chip = lax.rem(z + k, zs)
                both = pieces[half, pl.ds(2 * chip, 2)].reshape(2 * some, deep_k)
                terms[half, pl.ds(2 * chip, 2)] = (
                    jnp.dot(both, p_ref[...], preferred_element_type=f32)
                    .astype(bf16)
                    .reshape(2, some, model)
                )
                c = rc(
                    terms.at[half, mate_far[k]], near.at[half, k], s1.at[half, k], r1.at[half, k],
                    col=mate,
                )
                c.start()
                sent.append(c)
                if j:
                    combine(order[j - 1])
            combine(order[-1])
        for half in range(halves):
            rows = slice(half * some, (half + 1) * some)
            tot = sums[rows, :]
            for k in order[::-1][1:]:
                rc(
                    stage.at[half, 0], far_in.at[half, k], s2.at[half, k], r2.at[half, k], col=mate
                ).wait_recv()
                tot = tot + far_in[half, k].astype(f32)
            step = pos_ref.shape[0]
            for at in range(0, some, step):
                o_ref[half * some + at : half * some + at + step, :] = (
                    tot[at : at + step] + pos_ref[...].astype(f32)
                ).astype(bf16)
        for c in sent:
            c.wait_send()

    D = pltpu.SemaphoreType.DMA
    pad = -(-imgs * tall // 8) * 8
    return call(
        body,
        jax.ShapeDtypeStruct((tokens, model), bf16),
        [first.reshape(imgs * height, width, ch), conv, patch_weight, place_rows],
        [
            V((tokens, model), f32),
            V((2, imgs, width, ch), bf16),
            V((2, imgs * height, ch), f32),
            V((2, imgs * height, ch), bf16),
            V((2, imgs * height, ch), bf16),
            V((4, imgs, ch), bf16),
            V((4, imgs, ch), bf16),
            V((2, pad, ch), f32),
            V((3, imgs * tall, width, ch), bf16),
            V((ch // 128, imgs * height * width, 128), f32),
            V((n, tokens, deep_k), f32),
            V((halves, n, some, deep_k), bf16),
            V((halves, n, some, deep_k), bf16),
            V((halves, n, some, model), bf16),
        ]
        + [V((halves, zs, some, model), bf16)] * 3
        + [D((8,)), D((8,)), D((halves, n)), D((halves, n))]
        + [D((halves, zs))] * 4
        + [V(conv.shape, bf16), V(patch_weight.shape, bf16), D((2,))],
        cid,
        "stem",
        far=(1, 2),
    )


def layer_norm(vectors, gain_vec):
    row_mean = jnp.mean(vectors, axis=-1, keepdims=True)
    center = vectors - row_mean
    spread = jnp.mean(center * center, axis=-1, keepdims=True)
    return center * lax.rsqrt(spread + 1e-06) * gain_vec


def layer(x, gain_attn, w_qkv, w_out, gain_mlp, w_up, w_down, cols_here, per, cid):
    n, rows_n, secs = lax.axis_size("col"), lax.axis_size("row"), lax.axis_size("section")
    zs = n // 2
    width = x.shape[2]
    mine = x.shape[0] * x.shape[1]
    tokens = n * mine
    inner, hidden = w_out.shape[0], w_down.shape[0]
    heads = inner // HD
    chunks = 4
    piece = mine // chunks
    f32, bf16 = jnp.float32, jnp.bfloat16
    q_rows = math.gcd(tokens, 256)
    turned = per == 1 and cols_here % 8 == 0
    out_shape = (cols_here, mine // cols_here, width) if turned else (mine, width)

    def body(
        x_ref, g1_ref, g2_ref, wq_hbm, wo_hbm, wu_hbm, wd_hbm, o_ref,
        arrived, res, all1, all2, qkv, att, terms1, terms2,
        near1, stage1, far1, near2, stage2, far2,
        wq, wo, wu, wd, fetch,
        xs, xr, su1, sd1, sm1, ru1, rd1, rm1, su2, sd2, sm2, ru2, rd2, rm2,
        a1, b1, c1, d1, a2, b2, c2, d2,
    ):
        gets = []
        for j, (src, dst) in enumerate(((wq_hbm, wq), (wo_hbm, wo), (wu_hbm, wu), (wd_hbm, wd))):
            gets.append(pltpu.make_async_copy(src, dst, fetch.at[j]))
            gets[-1].start()
        sec, row, me = lax.axis_index("section"), lax.axis_index("row"), lax.axis_index("col")
        z, par = me // 2, lax.rem(me, 2)
        mate = me + 1 - 2 * par
        far = [lax.rem(me + 2 * k, n) for k in range(zs)]
        chips = [lax.rem(z + k, zs) for k in range(zs)]
        order = sorted(range(1, zs), key=lambda k: -min(k, zs - k)) + [0]
        to, back = lax.rem(sec + 1, secs), lax.rem(sec + secs - 1, secs)
        bar = pltpu.get_barrier_semaphore()

        def signal(dev):
            pl.semaphore_signal(bar, inc=1, device_id=dev, device_id_type=pl.DeviceIdType.MESH)

        signal({"col": mate})
        for k in range(1, zs):
            signal({"col": far[k]})
        for k in range(rows_n):
            signal({"section": back, "row": lax.rem(row + k, rows_n)})
        pl.semaphore_wait(bar, zs + rows_n)
        sent = []
        for k in range(rows_n):
            d = lax.rem(row + k, rows_n)
            c = rc(
                x_ref.at[d], arrived.at[row], xs.at[k], xr.at[(rows_n - k) % rows_n],
                section=to, row=d,
            )
            c.start()
            sent.append(c)
        for k in range(rows_n):
            d = lax.rem(row + k, rows_n)
            rc(x_ref.at[d], arrived.at[d], xs.at[k], xr.at[k], section=to, row=d).wait_recv()
        res[...] = arrived[...].reshape(mine, width).astype(f32)
        lo, hi = z > 0, z < zs - 1

        def gather(full, su, sd, sm, ru, rd, rm):
            def part(blk, c):
                return full.at[blk, pl.ds(c * piece, piece)]

            def up(blk, c):
                return rc(
                    part(blk, c), part(blk, c), su.at[blk // 2, c], ru.at[blk // 2, c], col=me + 2
                )

            def down(blk, c):
                return rc(
                    part(blk, c), part(blk, c), sd.at[blk // 2, c], rd.at[blk // 2, c], col=me - 2
                )

            def side(blk, c):
                return rc(
                    part(blk, c), part(blk, c), sm.at[blk // 2, c], rm.at[blk // 2, c], col=mate
                )

            for c in range(chunks):
                pl.when(hi)(lambda: up(me, c).start())
                pl.when(lo)(lambda: down(me, c).start())
            for c in range(chunks):
                side(me, c).start()
            for k in range(1, zs):
                for c in range(chunks):

                    @pl.when(z - k >= 0)
                    def _():
                        b = me - 2 * k
                        up(b, c).wait_recv()
                        pl.when(hi)(lambda: up(b, c).start())
                        side(b, c).start()

                    @pl.when(z + k < zs)
                    def _():
                        b = me + 2 * k
                        down(b, c).wait_recv()
                        pl.when(lo)(lambda: down(b, c).start())
                        side(b, c).start()

            for j in range(zs):
                for c in range(chunks):
                    b = 2 * j + par
                    side(b, c).wait_send()
                    side(2 * j + 1 - par, c).wait_recv()

                    @pl.when(hi & (j <= z))
                    def _():
                        up(b, c).wait_send()

                    @pl.when(lo & (j >= z))
                    def _():
                        down(b, c).wait_send()

        def scatter_sum(make, terms, near, stage, far_in, s1, r1, s2, r2):
            def combine(k):
                rc(terms.at[0], near.at[k], s1.at[k], r1.at[k], col=mate).wait_recv()
                tot = terms[far[k]].astype(f32) + near[k].astype(f32)
                if k:
                    stage[k] = tot.astype(bf16)
                    c = rc(stage.at[k], far_in.at[zs - k], s2.at[k], r2.at[zs - k], col=far[k])
                    c.start()
                    sent.append(c)
                return tot

            for j, k in enumerate(order):
                chip = chips[k]
                terms[pl.ds(2 * chip, 2)] = make(chip).astype(bf16).reshape(2, mine, width)
                c = rc(
                    terms.at[2 * chip + 1 - par], near.at[k], s1.at[k], r1.at[k], col=mate
                )
                c.start()
                sent.append(c)
                if j:
                    combine(order[j - 1])
            tot = combine(order[-1])
            for k in order[::-1][1:]:
                rc(stage.at[0], far_in.at[k], s2.at[k], r2.at[k], col=mate).wait_recv()
                tot = tot + far_in[k].astype(f32)
            return tot

        all1[me] = layer_norm(res[...], g1_ref[...]).astype(bf16)
        gather(all1, su1, sd1, sm1, ru1, rd1, rm1)
        gets[0].wait()
        every = all1[...].reshape(tokens, width)
        for j in range(3):
            qkv[j] = jnp.dot(every, wq[j], preferred_element_type=f32).astype(bf16)

        def attend(i, carry):
            at = pl.multiple_of(i * q_rows, q_rows)
            outs = []
            for h in range(heads):
                q = qkv[0, pl.ds(at, q_rows), h * HD : (h + 1) * HD]
                keys = qkv[1, :, h * HD : (h + 1) * HD]
                vals = qkv[2, :, h * HD : (h + 1) * HD]
                scores = lax.dot_general(
                    q, keys, (((1,), (1,)), ((), ())), preferred_element_type=f32
                ) * HD ** (-0.5)
                expo = jnp.exp(scores - jnp.max(scores, axis=-1, keepdims=True))
                probs = expo * (1.0 / jnp.sum(expo, axis=-1, keepdims=True))
                outs.append(jnp.dot(probs.astype(bf16), vals, preferred_element_type=f32))
            joined = outs[0] if heads == 1 else jnp.concatenate(outs, axis=-1)
            att[pl.ds(at, q_rows), :] = joined.astype(bf16)
            return carry

        lax.fori_loop(0, tokens // q_rows, attend, 0)
        gets[1].wait()

        def mixed(chip):
            rows = pl.ds(pl.multiple_of(chip * 2 * mine, 2 * mine), 2 * mine)
            return jnp.dot(att[rows, :], wo[...], preferred_element_type=f32)

        res[...] = res[...] + scatter_sum(mixed, terms1, near1, stage1, far1, a1, b1, c1, d1)
        all2[me] = layer_norm(res[...], g2_ref[...]).astype(bf16)
        gather(all2, su2, sd2, sm2, ru2, rd2, rm2)
        gets[2].wait()
        gets[3].wait()

        def mlp(chip):
            block = all2[pl.ds(2 * chip, 2)].reshape(2 * mine, width)
            mid = jax.nn.gelu(
                jnp.dot(block, wu[...], preferred_element_type=f32), approximate=True
            ).astype(bf16)
            return jnp.dot(mid, wd[...], preferred_element_type=f32)

        total = scatter_sum(mlp, terms2, near2, stage2, far2, a2, b2, c2, d2)
        done = res[...] + total
        if turned:
            done = done.reshape(mine // cols_here, cols_here, width).transpose(1, 0, 2)
        o_ref[...] = done.astype(bf16)
        for c in sent:
            c.wait_send()

    D = pltpu.SemaphoreType.DMA
    blocks = V((n, mine, width), bf16)
    quarter = V((zs, mine, width), bf16)
    return call(
        body,
        jax.ShapeDtypeStruct(out_shape, bf16),
        [x, gain_attn.reshape(1, -1), gain_mlp.reshape(1, -1), w_qkv, w_out, w_up, w_down],
        [
            V(x.shape, bf16),
            V((mine, width), f32),
            blocks,
            blocks,
            V((3, tokens, inner), bf16),
            V((tokens, inner), bf16),
            blocks,
            blocks,
        ]
        + [quarter] * 6
        + [V(w_qkv.shape, bf16), V(w_out.shape, bf16), V(w_up.shape, bf16), V(w_down.shape, bf16)]
        + [D((4,)), D((rows_n,)), D((rows_n,))]
        + [D((zs, chunks))] * 12
        + [D((zs,))] * 8,
        cid,
        "layer",
        far=(3, 4, 5, 6),
    )


def on_device(
    images,
    stem_first,
    stem_conv,
    patch_weight,
    position,
    gain_attn,
    w_qkv,
    w_out,
    gain_mlp,
    w_up,
    w_down,
):
    first_map = jnp.einsum(
        "ikhw,kc->ihwc", images[0], stem_first, preferred_element_type=jnp.float32
    )
    stem_maps = jnp.maximum(first_map, 0.0).astype(jnp.bfloat16)
    n = lax.axis_size("col")
    rows_n = lax.axis_size("row")
    model_width = patch_weight.shape[1]
    img_count, cols_here, rows_here = images.shape[1], images.shape[4] // 4, images.shape[3] // 4
    place_rows = position.transpose(1, 0, 2).reshape(-1, model_width)
    local_tokens = stem_embed(stem_maps, stem_conv, patch_weight, place_rows, 0)
    encoded = layer(
        local_tokens.reshape(rows_n, -1, model_width),
        gain_attn,
        w_qkv,
        w_out,
        gain_mlp,
        w_up,
        w_down,
        cols_here,
        img_count // rows_n,
        1,
    )
    per = img_count // rows_n
    if encoded.ndim == 2:
        encoded = encoded.reshape(rows_n, per, rows_here, cols_here, model_width).transpose(
            1, 3, 0, 2, 4
        )
    return encoded.reshape(1, per, cols_here, -1, model_width)


def solution(mesh):
    placed = (
        P("section", None, None, "row", "col"),
        P(),
        P(),
        P("col", None),
        P("col", "row", None),
        P(),
        P(None, None, "col"),
        P("col", None),
        P(),
        P(None, "col"),
        P("col", None),
    )
    return jax.shard_map(
        on_device,
        mesh=mesh,
        in_specs=placed,
        out_specs=P("section", "row", "col", None, None),
        check_vma=False,
    )
```
